32 devices in a mesh: zone: 4 (over y, x), dev: 8 (over z, core).
Axes of the slice: x: 2, y: 2, z: 4, core: 2. Of those that a mesh axis runs over, the one named last changes fastest.
Arguments:
- node_features: bfloat16 [16384, 512], P(('zone', 'dev')), may hold values from -9 to 9
- neighbour_blocks: int32 [128, 32], P(('zone', 'dev')), may hold values from 0 to 127, as said below
- neighbour_count: int32 [128], P(('zone', 'dev')), may hold values from 8 to 32, as said below
- tile_valid: int32 [128], replicated, may hold values from 64 to 128
- w_query: bfloat16 [512, 512], replicated, may hold values from -0.5 to 0.5
- w_key: bfloat16 [512, 512], replicated, may hold values from -0.5 to 0.5
- w_value: bfloat16 [512, 512], replicated, may hold values from -0.25 to 0.25
- w_out: bfloat16 [512, 512], replicated, may hold values from -0.25 to 0.25
- w_gate: bfloat16 [512, 2048], replicated, may hold values from -0.25 to 0.25
- w_up: bfloat16 [512, 2048], replicated, may hold values from -0.25 to 0.25
- w_down: bfloat16 [2048, 512], replicated, may hold values from -0.125 to 0.125
Outputs:
- layer_out: bfloat16 [16384, 512], P(('zone', 'dev'))
The draws below stay inside these ranges and needn't reach their ends.
Inputs may be any that keep to these rules, and one draw needn't show every extreme that they name: `neighbour_blocks`: each row lists 32 different blocks. Zones are runs of 32 blocks (zone of block g is g // 32); every listed block lies in the query block's zone or in one of the two zones beside it, counting around the last zone to the first. Each value is 8, 16 or 32, one value for each patch of 16 consecutive blocks (patch of block g is g // 16); only the first neighbour_count[b] slots of row b count.
All inputs are finite; a program needn't handle non-finite values.
Results may differ from the reference program's by a relative error of at most 0.007.
The reference program's roundings to bfloat16 on the way count: a program that leaves them out, or rounds other values in their place, can miss the bound.
Values may be sent and summed in bfloat16 or wider, within the bound.
No kernel may reach another device: no remote copies, remote signals or barrier semaphores. Data moves between devices by JAX's collectives and lax.ppermute only.
A program may use at most 448 MiB of HBM per device.

```python
import math
import jax
import jax.numpy as jnp
from jax import lax

D = 512
HEADS = 4
FF = 2048
TILE = 128
NB = 32
BLK_DEV = 4
BLOCKS = 128
NODES = 16384
N_ZONE = 4
N_DEV = 8


def draw_node_features(key, part):
    normal_part = jax.random.normal(jax.random.fold_in(key, 3), (NODES, D), jnp.float32)
    return jnp.clip(normal_part, -6.0, 6.0).astype(jnp.bfloat16)


def draw_neighbour_blocks(key, part):
    zone_blocks = BLK_DEV * N_DEV
    span = 3 * zone_blocks
    row_keys = jax.random.split(jax.random.fold_in(key, 11), BLOCKS)
    chosen = jax.vmap(lambda row_key: jax.random.permutation(row_key, span)[:NB])(row_keys)
    owner_zone = (jnp.arange(BLOCKS, dtype=jnp.int32) // zone_blocks)[:, None]
    zone_index = (owner_zone - 1 + chosen // zone_blocks) % N_ZONE
    return (zone_index * zone_blocks + chosen % zone_blocks).astype(jnp.int32)


def draw_neighbour_count(key, part):
    patch_blocks = 4 * BLK_DEV
    patch_total = BLOCKS // patch_blocks
    level_key, order_key = jax.random.split(jax.random.fold_in(key, 7))
    level = jax.random.randint(level_key, (patch_total,), 0, 3)
    order = jax.random.permutation(order_key, patch_total)
    level = level.at[order[0]].set(2).at[order[1]].set(0)
    counts = jnp.where(level == 0, NB // 4, jnp.where(level == 1, NB // 2, NB))
    return jnp.repeat(counts, patch_blocks).astype(jnp.int32)


def plant(values, own_key, smallest, top_value):
    index_at = [jax.random.randint(jax.random.fold_in(own_key, axis), (), 0, length) for axis, length in enumerate(values.shape)]
    widest = values.shape.index(max(values.shape))
    next_to = index_at[:widest] + [(index_at[widest] + 1) % values.shape[widest]] + index_at[widest + 1:]
    return values.at[tuple(index_at)].set(smallest).at[tuple(next_to)].set(top_value)


def noise(stream_key, dims, spread, bound, kind=jnp.bfloat16):
    values = jax.random.normal(stream_key, dims, jnp.float32) * spread
    return jnp.minimum(jnp.maximum(values, -bound), bound).astype(kind)


def setup_inputs(seed: int = 0) -> dict:
    splits = jax.random.split(jax.random.key(seed), 12)
    node_features = draw_node_features(jax.random.fold_in(splits[11], 71), 0)
    neighbour_blocks = draw_neighbour_blocks(jax.random.fold_in(splits[11], 71), 0)
    neighbour_count = draw_neighbour_count(jax.random.fold_in(splits[11], 71), 0)
    tile_valid = plant(jax.random.randint(splits[3], (BLOCKS,), TILE // 2, TILE + 1), jax.random.fold_in(splits[3], 1), TILE // 2, TILE).astype(jnp.int32)
    w_query = noise(splits[4], (D, D), (D // 4) ** -0.5, 0.5)
    w_key = noise(splits[5], (D, D), (D // 4) ** -0.5, 0.5)
    w_value = noise(splits[6], (D, D), D ** -0.5, 0.25)
    w_out = noise(splits[7], (D, D), D ** -0.5, 0.25)
    w_gate = noise(splits[8], (D, FF), D ** -0.5, 0.25)
    w_up = noise(splits[9], (D, FF), D ** -0.5, 0.25)
    w_down = noise(splits[10], (FF, D), FF ** -0.5, 0.125)
    return {"node_features": node_features, "neighbour_blocks": neighbour_blocks, "neighbour_count": neighbour_count, "tile_valid": tile_valid, "w_query": w_query, "w_key": w_key, "w_value": w_value, "w_out": w_out, "w_gate": w_gate, "w_up": w_up, "w_down": w_down}


def finish_layer(node_features, attended, w_out, w_gate, w_up, w_down):
    residual = node_features.astype(jnp.float32) + jnp.dot(attended, w_out, preferred_element_type=jnp.float32)
    inverse = lax.rsqrt(lax.optimization_barrier(jnp.mean(residual * residual, axis=-1, keepdims=True)) + 1e-06)
    normed = (residual * inverse).astype(jnp.bfloat16)
    gate_part = jnp.dot(normed, w_gate, preferred_element_type=jnp.float32)
    up_part = jnp.dot(normed, w_up, preferred_element_type=jnp.float32)
    hidden = (jax.nn.silu(gate_part) * up_part).astype(jnp.bfloat16)
    return (residual + jnp.dot(hidden, w_down, preferred_element_type=jnp.float32)).astype(jnp.bfloat16)

def reference(node_features, neighbour_blocks, neighbour_count, tile_valid, w_query, w_key, w_value, w_out, w_gate, w_up, w_down):
    head_dim = D // HEADS
    score_scale = 1.0 / math.sqrt(head_dim)
    queries = jnp.dot(node_features, w_query, preferred_element_type=jnp.float32).astype(jnp.bfloat16)
    key_rows = jnp.dot(node_features, w_key, preferred_element_type=jnp.float32).astype(jnp.bfloat16)
    value_rows = jnp.dot(node_features, w_value, preferred_element_type=jnp.float32).astype(jnp.bfloat16)
    queries, key_rows, value_rows = lax.optimization_barrier((queries, key_rows, value_rows))
    key_tiles = key_rows.reshape(BLOCKS, TILE, D)
    value_tiles = value_rows.reshape(BLOCKS, TILE, D)
    query_tiles = queries.reshape(BLOCKS, TILE, HEADS, head_dim)
    row_index = jnp.arange(TILE, dtype=jnp.int32)
    slot_index = jnp.arange(NB, dtype=jnp.int32)

    def one_block(block_item):
        query_tile, listed, live_count = block_item
        block_keys = jnp.take(key_tiles, listed, axis=0).reshape(NB * TILE, HEADS, head_dim).astype(jnp.float32)
        block_values = jnp.take(value_tiles, listed, axis=0).reshape(NB * TILE, HEADS, head_dim).astype(jnp.float32)
        valid_rows = jnp.take(tile_valid, listed)
        key_live = (slot_index < live_count)[:, None] & (row_index[None, :] < valid_rows[:, None])
        key_mask = key_live.reshape(1, 1, NB * TILE)
        scores = jnp.einsum('qhd,khd->hqk', query_tile.astype(jnp.float32), block_keys) * score_scale
        peak = lax.optimization_barrier(jnp.max(jnp.where(key_mask, scores, -1e+30), axis=-1, keepdims=True))
        weights = jnp.where(key_mask, jnp.exp(scores - peak), 0.0)
        denominator = lax.optimization_barrier(jnp.sum(weights, axis=-1))
        rounded = lax.optimization_barrier(weights.astype(jnp.bfloat16))
        summed = jnp.einsum('hqk,khd->qhd', rounded.astype(jnp.float32), block_values)
        return (summed / jnp.transpose(denominator)[:, :, None]).reshape(TILE, D).astype(jnp.bfloat16)
    attended = lax.map(one_block, (query_tiles, neighbour_blocks, neighbour_count)).reshape(NODES, D)
    return finish_layer(node_features, attended, w_out, w_gate, w_up, w_down)
```

```python
import functools
import math

import jax
import jax.numpy as jnp
from jax import lax
from jax.experimental import pallas as pl
from jax.experimental.pallas import tpu as pltpu
from jax.sharding import PartitionSpec as P

TILE = 128
HEADS = 4
LANES = 128
PAIR = 2 * LANES
AUG = LANES + 16
NEG = -1e30
BF = jnp.bfloat16
F32 = jnp.float32


def dot(a, b):
    return jnp.dot(a, b, preferred_element_type=F32)


def dot_t(a, b):
    return lax.dot_general(a, b, (((1,), (1,)), ((), ())), preferred_element_type=F32)


def whole(memory_space=pltpu.VMEM):
    return pl.BlockSpec(memory_space=memory_space)


def query_kernel(own_ref, partner_ref, wq_t_ref, out_ref):
    blocks = own_ref.shape[0] // TILE
    for half, ref in enumerate((own_ref, partner_ref)):
        q_t = dot_t(wq_t_ref[...], ref[...]).astype(BF)
        zero = jnp.zeros((LANES, TILE), BF)
        for b in range(blocks):
            col = slice(b * TILE, (b + 1) * TILE)
            for pair in range(HEADS // 2):
                top = q_t[pair * PAIR : pair * PAIR + LANES, col]
                low = q_t[pair * PAIR + LANES : (pair + 1) * PAIR, col]
                slot = out_ref.at[half * blocks + b, pair]
                slot[:LANES, :LANES] = top
                slot[:LANES, LANES:] = zero
                slot[LANES:, :LANES] = zero
                slot[LANES:, LANES:] = low


def make_queries(own, partner, wq_t):
    blocks = 2 * own.shape[0] // TILE
    return pl.pallas_call(
        query_kernel,
        out_shape=jax.ShapeDtypeStruct((blocks, HEADS // 2, PAIR, PAIR), BF),
        in_specs=[whole()] * 3,
        out_specs=whole(),
        compiler_params=pltpu.CompilerParams(vmem_limit_bytes=16 << 20),
        cost_estimate=pl.CostEstimate(
            flops=2 * 2 * own.shape[0] * own.shape[1] ** 2,
            bytes_accessed=4 << 20,
            transcendentals=0,
        ),
        name="queries",
    )(own, partner, wq_t)


def attend_kernel(n_slabs, base, blocks, factor, first, *refs):
    mem_ref, valid_ref = refs[:2]
    slabs = refs[2 : 2 + n_slabs]
    wk_hbm, wv_t_hbm, q_hbm = refs[2 + n_slabs : 5 + n_slabs]
    rest = refs[5 + n_slabs :]
    if not first:
        rest = rest[4:]
    outs, rest = rest[:4], rest[4:]
    bufs, rest = rest[:4], rest[4:]
    states = ((bufs[0], bufs[1]), (bufs[2], bufs[3]))
    wk_ref, wv_t_ref, q_ref, x_buf, k_buf, v_buf, list_k, list_v, list_q, sems = rest
    key_blocks = n_slabs * blocks
    moves = [(slabs[i], x_buf.at[i]) for i in range(n_slabs)]
    moves += [(wk_hbm, wk_ref), (wv_t_hbm, wv_t_ref), (q_hbm, q_ref)]
    if not first:
        moves += list(zip(outs, bufs))
    loads = [pltpu.make_async_copy(a, b, sems.at[i]) for i, (a, b) in enumerate(moves)]
    for load in loads:
        load.start()
    if first:
        for acc, top in states:
            acc[...] = jnp.zeros_like(acc)
            top[...] = jnp.full_like(top, NEG)
    v_buf[key_blocks] = jnp.zeros(v_buf.shape[1:], BF)

    counts = []
    for stream in range(2):
        pos = jnp.int32(0)
        for b in range(blocks):
            for k in range(key_blocks):
                list_k[stream, pos] = k
                list_v[stream, pos] = k
                list_q[stream, pos // 2] = b
                pos = pos + mem_ref[stream * blocks + b, base + k]
            odd = pos % 2
            list_k[stream, pos] = list_k[stream, jnp.maximum(pos - 1, 0)]
            list_v[stream, pos] = key_blocks
            pos = pos + odd
        counts.append(pos // 2)
    steps = jnp.maximum(counts[0], counts[1])
    for stream in range(2):

        def fill(i, carry, stream=stream):
            list_k[stream, 2 * i] = 0
            list_k[stream, 2 * i + 1] = 0
            list_v[stream, 2 * i + 1] = key_blocks
            list_q[stream, i] = blocks
            return carry

        lax.fori_loop(counts[stream], steps, fill, 0)

    for load in loads[: n_slabs + 2]:
        load.wait()

    def project(i, carry):
        x = x_buf.at[i]
        row = lax.broadcasted_iota(jnp.int32, (TILE, x.shape[1]), 0)
        lane = lax.broadcasted_iota(jnp.int32, (AUG - LANES, TILE), 1)
        filled, zeroed = [], []
        for j in range(blocks):
            valid = valid_ref[base + i * blocks + j]
            keep = jnp.where(row < valid, 1.0, 0.0).astype(BF)
            tile = x[j * TILE : (j + 1) * TILE, :]
            part = tile * keep
            zeroed.append(part)
            filled.append(part + tile[0:1, :] * (1 - keep))
            ones = jnp.where(lane < valid, 1.0, 0.0).astype(BF)
            for h in range(HEADS):
                v_buf[i * blocks + j, h, LANES:, :] = ones
        keys = dot(jnp.concatenate(filled, 0), wk_ref[...]).astype(BF)
        vals = dot_t(wv_t_ref[...], jnp.concatenate(zeroed, 0)).astype(BF)
        for j in range(blocks):
            k_buf[i * blocks + j] = keys[j * TILE : (j + 1) * TILE, :]
            for h in range(HEADS):
                v_buf[i * blocks + j, h, :LANES, :] = vals[
                    h * LANES : (h + 1) * LANES, j * TILE : (j + 1) * TILE
                ]
        return carry

    lax.fori_loop(0, n_slabs, project, 0)
    for load in loads[n_slabs + 2 :]:
        load.wait()

    def step(i, carry):
        jobs = []
        for stream, (acc, top) in enumerate(states):
            b = list_q[stream, i]
            k0 = list_k[stream, 2 * i]
            k1 = list_k[stream, 2 * i + 1]
            v1 = list_v[stream, 2 * i + 1]
            qi = jnp.minimum(b, blocks - 1) + stream * blocks
            for pair in range(HEADS // 2):
                cols = slice(pair * PAIR, (pair + 1) * PAIR)
                q = q_ref[qi, pair]
                s0 = dot(k_buf[k0, :, cols], q)
                s1 = dot(k_buf[k1, :, cols], q)
                jobs.append((acc, top, b, k0, v1, pair, cols, s0, s1))
        for acc, top, b, k0, v1, pair, cols, s0, s1 in jobs:
            old = top[b, 0:1, cols]
            peak = jnp.max(jnp.maximum(s0, s1), axis=0, keepdims=True)
            new = jnp.maximum(old, peak)
            scale = jnp.exp2((old - new) * factor)
            p0 = jnp.exp2((s0 - new) * factor).astype(BF)
            p1 = jnp.exp2((s1 - new) * factor).astype(BF)
            top[b, 0:1, cols] = new
            for side in range(2):
                h = pair * 2 + side
                sub = slice(side * LANES, (side + 1) * LANES)
                p = jnp.concatenate([p0[:, sub], p1[:, sub]], axis=0)
                v = jnp.concatenate([v_buf[k0, h], v_buf[v1, h]], axis=1)
                acc[b, h] = acc[b, h] * scale[:, sub] + dot(v, p)
        return carry

    lax.fori_loop(0, steps, step, 0)
    stores = [pltpu.make_async_copy(b, a, sems.at[i]) for i, (a, b) in enumerate(zip(outs, bufs))]
    for store in stores:
        store.start()
    for store in stores:
        store.wait()


def attend(slabs, base, tables, wk, wv_t, queries, factor, state):
    mem, valid = tables
    rows, width = slabs[0].shape
    blocks = rows // TILE
    n = len(slabs)
    key_blocks = n * blocks
    first = state is None
    state_shapes = [
        jax.ShapeDtypeStruct((blocks + 1, HEADS, AUG, TILE), F32),
        jax.ShapeDtypeStruct((blocks + 1, 8, HEADS * LANES), F32),
    ] * 2
    operands = [mem, valid, *slabs, wk, wv_t, queries]
    in_specs = [whole(pltpu.SMEM)] * 2 + [whole(pl.ANY)] * (n + 3)
    aliases = {}
    if not first:
        aliases = {len(operands) + i: i for i in range(4)}
        operands += list(state)
        in_specs += [whole(pl.ANY)] * 4
    slots = blocks * (key_blocks + 2) + 4
    return pl.pallas_call(
        functools.partial(attend_kernel, n, base, blocks, factor, first),
        out_shape=state_shapes,
        in_specs=in_specs,
        out_specs=[whole(pl.ANY)] * 4,
        input_output_aliases=aliases,
        scratch_shapes=[pltpu.VMEM(a.shape, a.dtype) for a in state_shapes]
        + [
            pltpu.VMEM(wk.shape, BF),
            pltpu.VMEM(wv_t.shape, BF),
            pltpu.VMEM(queries.shape, BF),
            pltpu.VMEM((n, rows, width), BF),
            pltpu.VMEM((key_blocks, TILE, width), BF),
            pltpu.VMEM((key_blocks + 1, HEADS, AUG, TILE), BF),
            pltpu.SMEM((2, slots), jnp.int32),
            pltpu.SMEM((2, slots), jnp.int32),
            pltpu.SMEM((2, slots), jnp.int32),
            pltpu.SemaphoreType.DMA((n + 7,)),
        ],
        compiler_params=pltpu.CompilerParams(vmem_limit_bytes=24 << 20),
        cost_estimate=pl.CostEstimate(
            flops=n * 2_000_000_000, bytes_accessed=8 << 20, transcendentals=0
        ),
        name="attend",
    )(*operands)


def finish_kernel(
    factor,
    acc_ref,
    top_ref,
    acc2_ref,
    top2_ref,
    x_ref,
    wo_hbm,
    wg_hbm,
    wu_hbm,
    wd_hbm,
    out_ref,
    att,
    wo,
    wg,
    wu,
    wd,
    sems,
):
    loads = [
        pltpu.make_async_copy(src, dst, sems.at[i])
        for i, (src, dst) in enumerate(
            ((wo_hbm, wo), (wg_hbm, wg), (wu_hbm, wu), (wd_hbm, wd))
        )
    ]
    for load in loads:
        load.start()
    rows, width = x_ref.shape
    for b in range(rows // TILE):
        for h in range(HEADS):
            cols = slice(h * LANES, (h + 1) * LANES)
            m1 = top_ref[b, 0:1, cols]
            m2 = top2_ref[b, 0:1, cols]
            m = jnp.maximum(m1, m2)
            a1 = jnp.exp2((m1 - m) * factor)
            a2 = jnp.exp2((m2 - m) * factor)
            den = acc_ref[b, h, LANES : LANES + 1, :] * a1 + acc2_ref[b, h, LANES : LANES + 1, :] * a2
            num = acc_ref[b, h, :LANES, :] * a1 + acc2_ref[b, h, :LANES, :] * a2
            att[b * TILE : (b + 1) * TILE, cols] = (num / den).T.astype(BF)
    loads[0].wait()
    residual = x_ref[...].astype(F32) + dot(att[...], wo[...])
    inverse = lax.rsqrt(jnp.mean(residual * residual, axis=-1, keepdims=True) + 1e-06)
    normed = (residual * inverse).astype(BF)
    for load in loads[1:]:
        load.wait()
    total = residual
    ff = wg.shape[1]
    for start in range(0, ff, 512):
        cols = slice(start, min(start + 512, ff))
        gate = dot(normed, wg[:, cols])
        up = dot(normed, wu[:, cols])
        hidden = (gate / (1.0 + jnp.exp(-gate)) * up).astype(BF)
        total = total + dot(hidden, wd[cols, :])
    out_ref[...] = total.astype(BF)


def finish(mine, theirs, x, w_out, w_gate, w_up, w_down, factor):
    rows, width = x.shape
    ff = w_gate.shape[1]
    return pl.pallas_call(
        functools.partial(finish_kernel, factor),
        out_shape=jax.ShapeDtypeStruct(x.shape, BF),
        in_specs=[whole()] * 5 + [whole(pl.ANY)] * 4,
        out_specs=whole(),
        scratch_shapes=[
            pltpu.VMEM((rows, width), BF),
            pltpu.VMEM(w_out.shape, BF),
            pltpu.VMEM(w_gate.shape, BF),
            pltpu.VMEM(w_up.shape, BF),
            pltpu.VMEM(w_down.shape, BF),
            pltpu.SemaphoreType.DMA((4,)),
        ],
        compiler_params=pltpu.CompilerParams(vmem_limit_bytes=32 << 20),
        cost_estimate=pl.CostEstimate(
            flops=2 * rows * width * (width + 3 * ff), bytes_accessed=12 << 20, transcendentals=0
        ),
        name="finish",
    )(*mine, *theirs, x, w_out, w_gate, w_up, w_down)


def pairs(zones, devs, move):
    out = []
    for zone in range(zones):
        for dev in range(devs):
            to = move(zone, dev)
            if to is not None:
                out.append((zone * devs + dev, to[0] * devs + to[1]))
    return out


def send(x, zones, devs, move):
    return lax.ppermute(x, ("zone", "dev"), pairs(zones, devs, move))


def gather_slabs(x, zones, devs):
    zone = lax.axis_index("zone")
    dev = lax.axis_index("dev")
    chips = devs // 2
    go = functools.partial(send, zones=zones, devs=devs)
    if zones == 4 and chips == 4:
        near = lambda a: go(a, move=lambda z, d: (z ^ 1, d))
        relay = lambda a: go(a, move=lambda z, d: (z ^ 2, d))
        middle = lambda a: go(a, move=lambda z, d: (z, d ^ 6) if d // 2 in (1, 2) else None)
        outer = lambda a: go(a, move=lambda z, d: (z, d ^ 2) if d // 2 in (1, 2) else None)
        edge = (dev // 2 == 0) | (dev // 2 == 3)
        a0 = x
        a1 = go(x, move=lambda z, d: (z, d ^ 2))
        n0 = near(a0)
        p2 = middle(x)
        f0 = relay(n0)
        n1 = near(a1)
        p3 = middle(a1)
        a2 = jnp.where(edge, outer(p2), p2)
        f1 = relay(n1)
        n2 = near(a2)
        a3 = jnp.where(edge, outer(p3), p3)
        f2 = relay(n2)
        n3 = near(a3)
        f3 = relay(n3)
        d0, d1 = dev, dev ^ 2
        d2 = jnp.where(edge, dev ^ 4, dev ^ 6)
        d3 = jnp.where(edge, dev ^ 6, dev ^ 4)
        nz, fz = zone ^ 1, zone ^ 3
        return [
            [(a0, zone, d0)],
            [(a1, zone, d1), (n0, nz, d0)],
            [(a2, zone, d2), (n1, nz, d1), (f0, fz, d0)],
            [(a3, zone, d3), (n2, nz, d2), (f1, fz, d1)],
            [(n3, nz, d3), (f2, fz, d2)],
            [(f3, fz, d3)],
        ]
    ahead = lax.ppermute(x, "zone", [(i, (i + 1) % zones) for i in range(zones)])
    behind = lax.ppermute(x, "zone", [((i + 1) % zones, i) for i in range(zones)])
    same_core = [[d for d in range(devs) if d % 2 == c] for c in range(2)]
    groups = []
    for slab, where in ((x, zone), (ahead, (zone - 1) % zones), (behind, (zone + 1) % zones)):
        every = lax.all_gather(slab, "dev", axis=0, axis_index_groups=same_core)
        for start in range(0, chips, 2):
            groups.append(
                [(every[c], where, 2 * c + dev % 2) for c in range(start, min(start + 2, chips))]
            )
    return groups


def body(
    node_features,
    neighbour_blocks,
    neighbour_count,
    tile_valid,
    w_query,
    w_key,
    w_value,
    w_out,
    w_gate,
    w_up,
    w_down,
):
    rows, width = node_features.shape
    blocks = rows // TILE
    zones, devs = lax.axis_size("zone"), lax.axis_size("dev")
    zone_blocks = blocks * devs
    factor = math.log2(math.e) / math.sqrt(width // HEADS)
    go = functools.partial(send, zones=zones, devs=devs)
    swap = lambda a: go(a, move=lambda z, d: (z, d ^ 1))

    slot = jnp.arange(neighbour_blocks.shape[1], dtype=jnp.int32)
    listed = jnp.where(slot[None, :] < neighbour_count[:, None], neighbour_blocks, -1)
    partner = swap(node_features)
    listed = jnp.concatenate([listed, swap(listed)], axis=0)

    groups = gather_slabs(node_features, zones, devs)
    ids = jnp.concatenate(
        [
            z * zone_blocks + d * blocks + jnp.arange(blocks, dtype=jnp.int32)
            for group in groups
            for _, z, d in group
        ]
    )
    mem = jnp.any(listed[:, :, None] == ids[None, None, :], axis=1).astype(jnp.int32)
    every = jnp.arange(tile_valid.shape[0], dtype=jnp.int32)
    valid = jnp.sum(jnp.where(ids[:, None] == every[None, :], tile_valid[None, :], 0), axis=1)

    queries = make_queries(node_features, partner, w_query.T)
    wv_t = w_value.T
    state, base = None, 0
    for group in groups:
        slabs = [s for s, _, _ in group]
        state = attend(slabs, base, (mem, valid), w_key, wv_t, queries, factor, state)
        base += len(slabs) * blocks
    theirs = [swap(state[2]), swap(state[3])]
    return finish(state[:2], theirs, node_features, w_out, w_gate, w_up, w_down, factor)


def solution(mesh):
    placed = (
        P(("zone", "dev"), None),
        P(("zone", "dev"), None),
        P(("zone", "dev")),
        P(),
        P(),
        P(),
        P(),
        P(),
        P(),
        P(),
        P(),
    )
    return jax.shard_map(
        body, mesh=mesh, in_specs=placed, out_specs=P(("zone", "dev"), None), check_vma=False
    )
```

```python
import functools
import math

import jax
import jax.numpy as jnp
from jax import lax
from jax.experimental import pallas as pl
from jax.experimental.pallas import tpu as pltpu
from jax.sharding import PartitionSpec as P


TILE = 128
HEADS = 4
LANES = 128
PAIR = 2 * LANES
AUG = LANES + 16
NEG = -1e30
ATTEND_LIMIT = 20
FINISH_LIMIT = 24
BF = jnp.bfloat16
F32 = jnp.float32


def dot(a, b):
    return jnp.dot(a, b, preferred_element_type=F32)


def dot_t(a, b):
    return lax.dot_general(a, b, (((1,), (1,)), ((), ())), preferred_element_type=F32)


def whole(memory_space=pltpu.VMEM):
    return pl.BlockSpec(memory_space=memory_space)


def query_kernel(own_ref, partner_ref, wq_ref, wv_ref, out_ref, wv_t_ref):
    blocks = own_ref.shape[0] // TILE
    wv_t_ref[...] = wv_ref[...].T
    wq_t = wq_ref[...].T
    for half, ref in enumerate((own_ref, partner_ref)):
        q_t = dot_t(wq_t, ref[...]).astype(BF)
        zero = jnp.zeros((LANES, TILE), BF)
        for b in range(blocks):
            col = slice(b * TILE, (b + 1) * TILE)
            for pair in range(HEADS // 2):
                top = q_t[pair * PAIR : pair * PAIR + LANES, col]
                low = q_t[pair * PAIR + LANES : (pair + 1) * PAIR, col]
                slot = out_ref.at[half * blocks + b, pair]
                slot[:LANES, :LANES] = top
                slot[:LANES, LANES:] = zero
                slot[LANES:, :LANES] = zero
                slot[LANES:, LANES:] = low


def make_queries(own, partner, wq, wv):
    blocks = 2 * own.shape[0] // TILE
    return pl.pallas_call(
        query_kernel,
        out_shape=[
            jax.ShapeDtypeStruct((blocks, HEADS // 2, PAIR, PAIR), BF),
            jax.ShapeDtypeStruct(wv.shape, BF),
        ],
        in_specs=[whole()] * 4,
        out_specs=[whole()] * 2,
        compiler_params=pltpu.CompilerParams(vmem_limit_bytes=16 << 20),
        cost_estimate=pl.CostEstimate(
            flops=2 * 2 * own.shape[0] * own.shape[1] ** 2,
            bytes_accessed=4 << 20,
            transcendentals=0,
        ),
        name="queries",
    )(own, partner, wq, wv)


def table_kernel(plan, blocks, slots, count_ref, valid_ref, own_ref, partner_ref, out_ref, *scratch):
    listed, member, flat, sem = scratch
    groups = plan(lax.axis_index("zone"), lax.axis_index("dev"))
    zone_blocks = blocks * lax.axis_size("dev")
    rows, width = own_ref.shape
    row = lax.broadcasted_iota(jnp.int32, (rows, width), 0)
    lane = lax.broadcasted_iota(jnp.int32, (rows, width), 1)
    count = jnp.zeros((rows, width), jnp.int32)
    for r in range(rows):
        count = jnp.where(row == r, count_ref[r], count)
    listed[:rows, :] = jnp.where(lane < count, own_ref[...], -1)
    listed[rows:, :] = jnp.where(lane < count, partner_ref[...], -1)
    every = listed[...]
    wide = lax.broadcasted_iota(jnp.int32, member.shape, 1)
    found = jnp.zeros(member.shape, jnp.int32)
    k = 0
    ids = []
    for group in groups:
        ids.append([])
        for z, d in group:
            for j in range(blocks):
                block = z * zone_blocks + d * blocks + j
                hit = jnp.max(jnp.where(every == block, 1, 0), axis=1, keepdims=True)
                found = jnp.where(wide == k, hit, found)
                ids[-1].append(block)
                k += 1
    member[...] = found
    copy = pltpu.make_async_copy(member, flat, sem)
    copy.start()
    copy.wait()
    base = 0
    for g, group in enumerate(ids):
        ends = []
        for stream in range(2):
            start = stream * slots
            pos = jnp.int32(start)
            for b in range(blocks):
                for j in range(len(group)):
                    out_ref[g, pos] = j + 256 * b
                    pos = pos + flat[stream * blocks + b, base + j]
                out_ref[g, pos] = out_ref[g, jnp.maximum(pos - 1, start)] + 65536
                pos = pos + pos % 2
            ends.append(pos - start)
        steps = jnp.maximum(ends[0], ends[1]) // 2
        steps = steps + steps % 2
        for stream in range(2):

            def fill(i, carry, g=g, start=stream * slots):
                out_ref[g, start + 2 * i] = 256 * blocks
                out_ref[g, start + 2 * i + 1] = 256 * blocks + 65536
                return carry

            lax.fori_loop(ends[stream] // 2, steps + 1, fill, 0)
        out_ref[g, 2 * slots] = steps
        for j, block in enumerate(group):
            out_ref[g, 2 * slots + 1 + j] = valid_ref[block]
        base += len(group)


def make_tables(plan, sizes, blocks, counts, tile_valid, own, partner):
    slots = blocks * max(sizes) * blocks + 4
    width = 2 * slots + 1 + blocks * max(sizes)
    width += -width % LANES
    keys = sum(sizes) * blocks
    tables = pl.pallas_call(
        functools.partial(table_kernel, plan, blocks, slots),
        out_shape=jax.ShapeDtypeStruct((len(sizes), width), jnp.int32),
        in_specs=[whole(pltpu.SMEM)] * 2 + [whole()] * 2,
        out_specs=whole(pltpu.SMEM),
        scratch_shapes=[
            pltpu.VMEM((2 * blocks, own.shape[1]), jnp.int32),
            pltpu.VMEM((2 * blocks, keys + -keys % LANES), jnp.int32),
            pltpu.SMEM((2 * blocks, keys + -keys % LANES), jnp.int32),
            pltpu.SemaphoreType.DMA,
        ],
        compiler_params=pltpu.CompilerParams(vmem_limit_bytes=8 << 20),
        cost_estimate=pl.CostEstimate(flops=10_000_000, bytes_accessed=1 << 20, transcendentals=0),
        name="tables",
    )(counts, tile_valid, own, partner)
    return tables, slots


def pick_kernel(edge_ref, inner_ref, out_ref):
    chip = lax.axis_index("dev") // 2
    at_edge = (chip == 0) | (chip == lax.axis_size("dev") // 2 - 1)

    @pl.when(at_edge)
    def _():
        out_ref[...] = edge_ref[...]

    @pl.when(jnp.logical_not(at_edge))
    def _():
        out_ref[...] = inner_ref[...]


def pick(at_edge, inner):
    return pl.pallas_call(
        pick_kernel,
        out_shape=jax.ShapeDtypeStruct(inner.shape, inner.dtype),
        in_specs=[whole()] * 2,
        out_specs=whole(),
        compiler_params=pltpu.CompilerParams(vmem_limit_bytes=8 << 20),
        cost_estimate=pl.CostEstimate(flops=0, bytes_accessed=1 << 20, transcendentals=0),
        name="pick",
    )(at_edge, inner)


def attend_kernel(n_slabs, group, slots, blocks, factor, first, *refs):
    table = refs[0]
    slabs = refs[1 : 1 + n_slabs]
    wk_ref, wv_t_ref, q_ref = refs[1 + n_slabs : 4 + n_slabs]
    rest = refs[4 + n_slabs :]
    olds, rest = ([], rest) if first else (rest[:4], rest[4:])
    outs, rest = rest[:4], rest[4:]
    states = ((outs[0], outs[1]), (outs[2], outs[3]))
    k_buf, v_buf, s_even, s_odd, peak_even, peak_odd = rest
    key_blocks = n_slabs * blocks
    if first:
        for acc, top in states:
            acc[...] = jnp.zeros_like(acc)
            top[...] = jnp.full_like(top, NEG)
    for old, out in zip(olds, outs):
        out[...] = old[...]
    v_buf[key_blocks] = jnp.zeros(v_buf.shape[1:], BF)

    def entry(stream, i):
        e0 = table[group, stream * slots + 2 * i]
        e1 = table[group, stream * slots + 2 * i + 1]
        k0, k1 = e0 & 255, e1 & 255
        return (e0 >> 8) & 255, k0, k1, jnp.where(e1 >= 65536, key_blocks, k1)

    for i, x in enumerate(slabs):
        row = lax.broadcasted_iota(jnp.int32, (TILE, x.shape[1]), 0)
        lane = lax.broadcasted_iota(jnp.int32, (AUG - LANES, TILE), 1)
        filled, zeroed = [], []
        for j in range(blocks):
            valid = table[group, 2 * slots + 1 + i * blocks + j]
            keep = jnp.where(row < valid, 1.0, 0.0).astype(BF)
            tile = x[j * TILE : (j + 1) * TILE, :]
            part = tile * keep
            zeroed.append(part)
            filled.append(part + tile[0:1, :] * (1 - keep))
            ones = jnp.where(lane < valid, 1.0, 0.0).astype(BF)
            for h in range(HEADS):
                v_buf[i * blocks + j, h, LANES:, :] = ones
        keys = dot(jnp.concatenate(filled, 0), wk_ref[...]).astype(BF)
        vals = dot_t(wv_t_ref[...], jnp.concatenate(zeroed, 0)).astype(BF)
        for j in range(blocks):
            k_buf[i * blocks + j] = keys[j * TILE : (j + 1) * TILE, :]
            for h in range(HEADS):
                v_buf[i * blocks + j, h, :LANES, :] = vals[
                    h * LANES : (h + 1) * LANES, j * TILE : (j + 1) * TILE
                ]

    def score(i, buf, peaks):
        for stream in range(2):
            b, k0, k1, _ = entry(stream, i)
            qi = jnp.minimum(b, blocks - 1) + stream * blocks
            for pair in range(HEADS // 2):
                cols = slice(pair * PAIR, (pair + 1) * PAIR)
                q = q_ref[qi, pair]
                s0 = dot(k_buf[k0, :, cols], q)
                s1 = dot(k_buf[k1, :, cols], q)
                buf[stream, pair, 0] = s0
                buf[stream, pair, 1] = s1
                peaks[stream, 0:1, cols] = jnp.max(
                    jnp.maximum(s0, s1), axis=0, keepdims=True
                )

    def update(i, buf, peaks):
        for stream, (acc, top) in enumerate(states):
            b, k0, _, v1 = entry(stream, i)
            old = top[b, 0:1, :]
            new = jnp.maximum(old, peaks[stream, 0:1, :])
            scale = jnp.exp2((old - new) * factor)
            top[b, 0:1, :] = new
            for pair in range(HEADS // 2):
                high = new[:, pair * PAIR : (pair + 1) * PAIR]
                p0 = jnp.exp2((buf[stream, pair, 0] - high) * factor).astype(BF)
                p1 = jnp.exp2((buf[stream, pair, 1] - high) * factor).astype(BF)
                for side in range(2):
                    h = pair * 2 + side
                    sub = slice(side * LANES, (side + 1) * LANES)
                    p = jnp.concatenate([p0[:, sub], p1[:, sub]], axis=0)
                    v = jnp.concatenate([v_buf[k0, h], v_buf[v1, h]], axis=1)
                    part = scale[:, h * LANES : (h + 1) * LANES]
                    acc[b, h] = acc[b, h] * part + dot(v, p)

    score(0, s_even, peak_even)

    def two(i, carry):
        score(2 * i + 1, s_odd, peak_odd)
        update(2 * i, s_even, peak_even)
        score(2 * i + 2, s_even, peak_even)
        update(2 * i + 1, s_odd, peak_odd)
        return carry

    lax.fori_loop(0, table[group, 2 * slots] // 2, two, 0)


def attend(slabs, group, tables, wk, wv_t, queries, factor, state):
    table, slots = tables
    rows, width = slabs[0].shape
    blocks = rows // TILE
    n = len(slabs)
    key_blocks = n * blocks
    first = state is None
    state_shapes = [
        jax.ShapeDtypeStruct((blocks + 1, HEADS, AUG, TILE), F32),
        jax.ShapeDtypeStruct((blocks + 1, 8, HEADS * LANES), F32),
    ] * 2
    operands = [table, *slabs, wk, wv_t, queries]
    in_specs = [whole(pltpu.SMEM)] + [whole()] * (n + 3)
    aliases = {}
    if not first:
        aliases = {len(operands) + i: i for i in range(4)}
        operands += list(state)
        in_specs += [whole()] * 4
    return pl.pallas_call(
        functools.partial(attend_kernel, n, group, slots, blocks, factor, first),
        out_shape=state_shapes,
        in_specs=in_specs,
        out_specs=[whole()] * 4,
        input_output_aliases=aliases,
        scratch_shapes=[
            pltpu.VMEM((key_blocks, TILE, width), BF),
            pltpu.VMEM((key_blocks + 1, HEADS, AUG, TILE), BF),
            pltpu.VMEM((2, HEADS // 2, 2, TILE, PAIR), F32),
            pltpu.VMEM((2, HEADS // 2, 2, TILE, PAIR), F32),
            pltpu.VMEM((2, 8, width), F32),
            pltpu.VMEM((2, 8, width), F32),
        ],
        compiler_params=pltpu.CompilerParams(vmem_limit_bytes=ATTEND_LIMIT << 20),
        cost_estimate=pl.CostEstimate(
            flops=n * 2_000_000_000, bytes_accessed=8 << 20, transcendentals=0
        ),
        name="attend",
    )(*operands)


def finish_kernel(
    factor,
    acc_ref,
    top_ref,
    acc2_ref,
    top2_ref,
    x_ref,
    wo_ref,
    wg_ref,
    wu_ref,
    wd_ref,
    out_ref,
    att,
):
    rows, _ = x_ref.shape
    for b in range(rows // TILE):
        for h in range(HEADS):
            cols = slice(h * LANES, (h + 1) * LANES)
            m1 = top_ref[b, 0:1, cols]
            m2 = top2_ref[b, 0:1, cols]
            m = jnp.maximum(m1, m2)
            a1 = jnp.exp2((m1 - m) * factor)
            a2 = jnp.exp2((m2 - m) * factor)
            den = (
                acc_ref[b, h, LANES : LANES + 1, :] * a1
                + acc2_ref[b, h, LANES : LANES + 1, :] * a2
            )
            num = acc_ref[b, h, :LANES, :] * a1 + acc2_ref[b, h, :LANES, :] * a2
            att[b * TILE : (b + 1) * TILE, cols] = (num / den).T.astype(BF)
    residual = x_ref[...].astype(F32) + dot(att[...], wo_ref[...])
    inverse = lax.rsqrt(jnp.mean(residual * residual, axis=-1, keepdims=True) + 1e-06)
    normed = (residual * inverse).astype(BF)
    total = residual
    ff = wg_ref.shape[1]
    for start in range(0, ff, 512):
        cols = slice(start, min(start + 512, ff))
        gate = dot(normed, wg_ref[:, cols])
        up = dot(normed, wu_ref[:, cols])
        hidden = (gate / (1.0 + jnp.exp(-gate)) * up).astype(BF)
        total = total + dot(hidden, wd_ref[cols, :])
    out_ref[...] = total.astype(BF)


def finish(mine, theirs, x, w_out, w_gate, w_up, w_down, factor):
    rows, width = x.shape
    ff = w_gate.shape[1]
    return pl.pallas_call(
        functools.partial(finish_kernel, factor),
        out_shape=jax.ShapeDtypeStruct(x.shape, BF),
        in_specs=[whole()] * 9,
        out_specs=whole(),
        scratch_shapes=[pltpu.VMEM((rows, width), BF)],
        compiler_params=pltpu.CompilerParams(vmem_limit_bytes=FINISH_LIMIT << 20),
        cost_estimate=pl.CostEstimate(
            flops=2 * rows * width * (width + 3 * ff), bytes_accessed=12 << 20, transcendentals=0
        ),
        name="finish",
    )(*mine, *theirs, x, w_out, w_gate, w_up, w_down)


def pairs(zones, devs, move):
    out = []
    for zone in range(zones):
        for dev in range(devs):
            to = move(zone, dev)
            if to is not None:
                out.append((zone * devs + dev, to[0] * devs + to[1]))
    return out


def send(x, zones, devs, move):
    return lax.ppermute(x, ("zone", "dev"), pairs(zones, devs, move))


def walks(zones, devs):
    return zones == 4 and devs == 8


def walk_plan(zone, dev):
    n, f = zone ^ 1, zone ^ 3
    return [
        [(zone, dev)],
        [(zone, dev ^ 2), (n, dev)],
        [(zone, dev ^ 4), (n, dev ^ 2), (f, dev)],
        [(zone, dev ^ 6), (n, dev ^ 4), (f, dev ^ 2)],
        [(n, dev ^ 6), (f, dev ^ 4), (f, dev ^ 6)],
    ]


def walk_links(x, zones, devs, work):
    go = functools.partial(send, zones=zones, devs=devs)
    near = lambda a: go(a, move=lambda z, d: (z ^ 1, d))
    relay = lambda a: go(a, move=lambda z, d: (z ^ 2, d))
    inner = lambda d: d // 2 in (1, 2)
    middle = lambda a: go(a, move=lambda z, d: (z, d ^ 6) if inner(d) else None)
    outer = lambda a: go(a, move=lambda z, d: (z, d ^ 2) if inner(d) else None)
    ends = lambda a: go(a, move=lambda z, d: (z, d ^ 6) if not inner(d) else None)

    a1 = go(x, move=lambda z, d: (z, d ^ 2))
    n0 = near(x)
    p2 = middle(x)
    work([x])
    p4 = outer(p2)
    n1 = near(a1)
    f0 = relay(n0)
    p3 = middle(a1)
    work([a1, n0])
    p5 = outer(p3)
    f1 = relay(n1)
    a2 = pick(p4, p3)
    n2 = near(a2)
    g_inner = middle(f0)
    work([a2, n1, f0])
    a3 = pick(p5, p2)
    n3 = near(a3)
    f2 = relay(n2)
    g_ends = ends(f0)
    work([a3, n2, f1])
    f3 = pick(g_ends, g_inner)
    work([n3, f2, f3])


def gather_plan(zone, dev, zones, devs):
    return [
        [(where, 2 * c + dev % 2) for c in range(start, min(start + 2, devs // 2))]
        for where in (zone, (zone - 1) % zones, (zone + 1) % zones)
        for start in range(0, devs // 2, 2)
    ]


def gather_zones(x, zones, devs, work):
    chips = devs // 2
    ahead = lax.ppermute(x, "zone", [(i, (i + 1) % zones) for i in range(zones)])
    behind = lax.ppermute(x, "zone", [((i + 1) % zones, i) for i in range(zones)])
    same_core = [[d for d in range(devs) if d % 2 == c] for c in range(2)]
    for slab in (x, ahead, behind):
        every = lax.all_gather(slab, "dev", axis=0, axis_index_groups=same_core)
        for start in range(0, chips, 2):
            work([every[c] for c in range(start, min(start + 2, chips))])


def body(
    node_features,
    neighbour_blocks,
    neighbour_count,
    tile_valid,
    w_query,
    w_key,
    w_value,
    w_out,
    w_gate,
    w_up,
    w_down,
):
    rows, width = node_features.shape
    blocks = rows // TILE
    zones, devs = lax.axis_size("zone"), lax.axis_size("dev")
    factor = math.log2(math.e) / math.sqrt(width // HEADS)
    go = functools.partial(send, zones=zones, devs=devs)
    swap = lambda a: go(a, move=lambda z, d: (z, d ^ 1))

    partner = swap(node_features)
    listed = swap(neighbour_blocks)
    if walks(zones, devs):
        plan, run = walk_plan, walk_links
    else:
        plan, run = functools.partial(gather_plan, zones=zones, devs=devs), gather_zones
    sizes = [len(group) for group in plan(0, 0)]
    tables = make_tables(
        plan, sizes, blocks, neighbour_count, tile_valid, neighbour_blocks, listed
    )
    queries, wv_t = make_queries(node_features, partner, w_query, w_value)
    state, turn = None, 0

    def work(slabs):
        nonlocal state, turn
        state = attend(slabs, turn, tables, w_key, wv_t, queries, factor, state)
        turn += 1

    run(node_features, zones, devs, work)
    theirs = [swap(state[2]), swap(state[3])]
    return finish(state[:2], theirs, node_features, w_out, w_gate, w_up, w_down, factor)


def solution(mesh):
    placed = (
        P(("zone", "dev"), None),
        P(("zone", "dev"), None),
        P(("zone", "dev")),
        P(),
        P(),
        P(),
        P(),
        P(),
        P(),
        P(),
        P(),
    )

    return jax.shard_map(
        body, mesh=mesh, in_specs=placed, out_specs=P(("zone", "dev"), None), check_vma=False
    )
```

```python
import functools
import math

import jax
import jax.numpy as jnp
from jax import lax
from jax.experimental import pallas as pl
from jax.experimental.pallas import tpu as pltpu
from jax.sharding import PartitionSpec as P


TILE = 128
HEADS = 4
LANES = 128
PAIR = 2 * LANES
AUG = LANES + 16
NEG = -1e30
ATTEND_LIMIT = 20
FINISH_LIMIT = 24
BF = jnp.bfloat16
F32 = jnp.float32


def dot(a, b):
    return jnp.dot(a, b, preferred_element_type=F32)


def dot_t(a, b):
    return lax.dot_general(a, b, (((1,), (1,)), ((), ())), preferred_element_type=F32)


def whole(memory_space=pltpu.VMEM):
    return pl.BlockSpec(memory_space=memory_space)


def fill_tables(groups, slots, width, blocks, count_ref, valid_ref, own_ref, partner_ref, out_ref, scratch):
    listed, member, flat, sem = scratch
    zone_blocks = blocks * lax.axis_size("dev")
    rows, slots_listed = own_ref.shape
    row = lax.broadcasted_iota(jnp.int32, (rows, slots_listed), 0)
    lane = lax.broadcasted_iota(jnp.int32, (rows, slots_listed), 1)
    count = jnp.zeros((rows, slots_listed), jnp.int32)
    for r in range(rows):
        count = jnp.where(row == r, count_ref[r], count)
    listed[:rows, :] = jnp.where(lane < count, own_ref[...], -1)
    listed[rows:, :] = jnp.where(lane < count, partner_ref[...], -1)
    every = listed[...]
    wide = lax.broadcasted_iota(jnp.int32, member.shape, 1)
    found = jnp.zeros(member.shape, jnp.int32)
    k = 0
    ids = []
    for group in groups:
        ids.append([])
        for z, d in group:
            for j in range(blocks):
                block = z * zone_blocks + d * blocks + j
                hit = jnp.max(jnp.where(every == block, 1, 0), axis=1, keepdims=True)
                found = jnp.where(wide == k, hit, found)
                ids[-1].append(block)
                k += 1
    member[...] = found
    copy = pltpu.make_async_copy(member, flat, sem)
    copy.start()
    copy.wait()
    base = 0
    for g, group in enumerate(ids):
        ends = []
        for stream in range(2):
            start = g * width + stream * slots
            pos = jnp.int32(start)
            for b in range(blocks):
                for j in range(len(group)):
                    out_ref[pos] = j + 256 * b
                    pos = pos + flat[stream * blocks + b, base + j]
                out_ref[pos] = out_ref[jnp.maximum(pos - 1, start)] + 65536
                pos = pos + ((pos - start) & 1)
            ends.append(pos - start)
        steps = jnp.maximum(ends[0], ends[1]) >> 1
        steps = steps + (steps & 1)
        for stream in range(2):

            def fill(i, carry, start=g * width + stream * slots):
                out_ref[start + 2 * i] = 256 * blocks
                out_ref[start + 2 * i + 1] = 256 * blocks + 65536
                return carry

            lax.fori_loop(ends[stream] >> 1, steps + 1, fill, 0)
        out_ref[g * width + 2 * slots] = steps
        for j, block in enumerate(group):
            out_ref[g * width + 2 * slots + 1 + j] = valid_ref[block]
        base += len(group)


def prepare_kernel(plan, blocks, slots, width, *refs):
    count_hbm, valid_hbm, own_list_hbm, partner_list_hbm, x_hbm, wq_hbm, wv_hbm, partner_ref = refs[:8]
    table_ref, out_ref, wv_t_ref = refs[8:11]
    count, valid, own_list, partner_list, x_ref, wq_ref, wv_ref = refs[11:18]
    scratch, sems = refs[18:22], refs[22]
    moves = (
        (count_hbm, count),
        (valid_hbm, valid),
        (own_list_hbm, own_list),
        (partner_list_hbm, partner_list),
        (wq_hbm, wq_ref),
        (x_hbm, x_ref),
        (wv_hbm, wv_ref),
    )
    loads = [pltpu.make_async_copy(a, b, sems.at[i]) for i, (a, b) in enumerate(moves)]
    for load in loads:
        load.start()
    for load in loads[:4]:
        load.wait()
    groups = plan(lax.axis_index("zone"), lax.axis_index("dev"))
    fill_tables(groups, slots, width, blocks, count, valid, own_list, partner_list, table_ref, scratch)
    for load in loads[4:]:
        load.wait()
    wv_t_ref[...] = wv_ref[...].T
    wq_t = wq_ref[...].T
    zero = jnp.zeros((LANES, TILE), BF)
    for half, ref in enumerate((x_ref, partner_ref)):
        q_t = dot_t(wq_t, ref[...]).astype(BF)
        for b in range(blocks):
            col = slice(b * TILE, (b + 1) * TILE)
            for pair in range(HEADS // 2):
                slot = out_ref.at[half * blocks + b, pair]
                slot[:LANES, :LANES] = q_t[pair * PAIR : pair * PAIR + LANES, col]
                slot[:LANES, LANES:] = zero
                slot[LANES:, :LANES] = zero
                slot[LANES:, LANES:] = q_t[pair * PAIR + LANES : (pair + 1) * PAIR, col]


def prepare(plan, sizes, counts, tile_valid, listed, partner_listed, x, partner, wq, wv):
    blocks = x.shape[0] // TILE
    slots = blocks * max(sizes) * blocks + 4
    width = 2 * slots + 1 + blocks * max(sizes)
    width += -width % LANES
    keys = sum(sizes) * blocks
    keys += -keys % LANES
    table, queries, wv_t = pl.pallas_call(
        functools.partial(prepare_kernel, plan, blocks, slots, width),
        out_shape=[
            jax.ShapeDtypeStruct((len(sizes) * width,), jnp.int32),
            jax.ShapeDtypeStruct((2 * blocks, HEADS // 2, PAIR, PAIR), BF),
            jax.ShapeDtypeStruct(wv.shape, BF),
        ],
        in_specs=[whole(pltpu.HBM)] * 3 + [whole(pl.ANY)] + [whole(pltpu.HBM)] * 3 + [whole()],
        out_specs=[whole(pltpu.SMEM), whole(), whole()],
        scratch_shapes=[
            pltpu.SMEM(counts.shape, jnp.int32),
            pltpu.SMEM(tile_valid.shape, jnp.int32),
            pltpu.VMEM(listed.shape, jnp.int32),
            pltpu.VMEM(listed.shape, jnp.int32),
            pltpu.VMEM(x.shape, BF),
            pltpu.VMEM(wq.shape, BF),
            pltpu.VMEM(wv.shape, BF),
            pltpu.VMEM((2 * blocks, listed.shape[1]), jnp.int32),
            pltpu.VMEM((2 * blocks, keys), jnp.int32),
            pltpu.SMEM((2 * blocks, keys), jnp.int32),
            pltpu.SemaphoreType.DMA,
            pltpu.SemaphoreType.DMA((7,)),
        ],
        compiler_params=pltpu.CompilerParams(vmem_limit_bytes=16 << 20),
        cost_estimate=pl.CostEstimate(
            flops=4 * x.shape[0] * x.shape[1] ** 2, bytes_accessed=4 << 20, transcendentals=0
        ),
        name="prepare",
    )(
        *[pltpu.with_memory_space_constraint(a, pltpu.HBM) for a in (counts, tile_valid, listed)],
        partner_listed,
        *[pltpu.with_memory_space_constraint(a, pltpu.HBM) for a in (x, wq, wv)],
        partner,
    )
    return (table, slots, width), queries, wv_t


def pick_kernel(edge_ref, inner_ref, out_ref):
    chip = lax.axis_index("dev") // 2
    at_edge = (chip == 0) | (chip == lax.axis_size("dev") // 2 - 1)

    @pl.when(at_edge)
    def _():
        out_ref[...] = edge_ref[...]

    @pl.when(jnp.logical_not(at_edge))
    def _():
        out_ref[...] = inner_ref[...]


def pick(at_edge, inner):
    return pl.pallas_call(
        pick_kernel,
        out_shape=jax.ShapeDtypeStruct(inner.shape, inner.dtype),
        in_specs=[whole()] * 2,
        out_specs=whole(),
        compiler_params=pltpu.CompilerParams(vmem_limit_bytes=8 << 20),
        cost_estimate=pl.CostEstimate(flops=0, bytes_accessed=1 << 20, transcendentals=0),
        name="pick",
    )(at_edge, inner)


def attend_kernel(n_slabs, base, slots, blocks, factor, first, last, *refs):
    table = refs[0]
    slabs = refs[1 : 1 + n_slabs]
    wk_ref, wv_t_ref, q_ref = refs[1 + n_slabs : 4 + n_slabs]
    rest = refs[4 + n_slabs :]
    olds, rest = ([], rest) if first else (rest[:4], rest[4:])
    outs, rest = rest[:4], rest[4:]
    if last:
        half_ref, stat_ref, rest = outs[2], outs[3], rest
        outs, rest = outs[:2] + rest[:2], rest[2:]
    states = ((outs[0], outs[1]), (outs[2], outs[3]))
    k_buf, v_buf, s_even, s_odd, peak_even, peak_odd = rest
    key_blocks = n_slabs * blocks
    if first:
        for acc, top in states:
            acc[...] = jnp.zeros_like(acc)
            top[...] = jnp.full_like(top, NEG)
    for old, out in zip(olds, outs):
        out[...] = old[...]
    v_buf[key_blocks] = jnp.zeros(v_buf.shape[1:], BF)

    def entry(stream, i):
        e0 = table[base + stream * slots + 2 * i]
        e1 = table[base + stream * slots + 2 * i + 1]
        k0, k1 = e0 & 255, e1 & 255
        return (e0 >> 8) & 255, k0, k1, jnp.where(e1 >= 65536, key_blocks, k1)

    for i, x in enumerate(slabs):
        row = lax.broadcasted_iota(jnp.int32, (TILE, x.shape[1]), 0)
        lane = lax.broadcasted_iota(jnp.int32, (AUG - LANES, TILE), 1)
        filled, zeroed = [], []
        for j in range(blocks):
            valid = table[base + 2 * slots + 1 + i * blocks + j]
            keep = jnp.where(row < valid, 1.0, 0.0).astype(BF)
            tile = x[j * TILE : (j + 1) * TILE, :]
            part = tile * keep
            zeroed.append(part)
            filled.append(part + tile[0:1, :] * (1 - keep))
            ones = jnp.where(lane < valid, 1.0, 0.0).astype(BF)
            for h in range(HEADS):
                v_buf[i * blocks + j, h, LANES:, :] = ones
        keys = dot(jnp.concatenate(filled, 0), wk_ref[...]).astype(BF)
        vals = dot_t(wv_t_ref[...], jnp.concatenate(zeroed, 0)).astype(BF)
        for j in range(blocks):
            k_buf[i * blocks + j] = keys[j * TILE : (j + 1) * TILE, :]
            for h in range(HEADS):
                v_buf[i * blocks + j, h, :LANES, :] = vals[
                    h * LANES : (h + 1) * LANES, j * TILE : (j + 1) * TILE
                ]

    def score(i, buf, peaks, stream, pair):
        b, k0, k1, _ = entry(stream, i)
        cols = slice(pair * PAIR, (pair + 1) * PAIR)
        q = q_ref[jnp.minimum(b, blocks - 1) + stream * blocks, pair]
        s0 = dot(k_buf[k0, :, cols], q)
        s1 = dot(k_buf[k1, :, cols], q)
        buf[stream, pair, 0] = s0
        buf[stream, pair, 1] = s1
        peaks[stream, 0:1, cols] = jnp.max(jnp.maximum(s0, s1), axis=0, keepdims=True)

    def update(i, buf, peaks, stream, pair):
        acc, top = states[stream]
        b, k0, _, v1 = entry(stream, i)
        cols = slice(pair * PAIR, (pair + 1) * PAIR)
        old = top[b, 0:1, cols]
        new = jnp.maximum(old, peaks[stream, 0:1, cols])
        scale = jnp.exp2((old - new) * factor)
        top[b, 0:1, cols] = new
        p0 = jnp.exp2((buf[stream, pair, 0] - new) * factor).astype(BF)
        p1 = jnp.exp2((buf[stream, pair, 1] - new) * factor).astype(BF)
        for side in range(2):
            h = pair * 2 + side
            sub = slice(side * LANES, (side + 1) * LANES)
            p = jnp.concatenate([p0[:, sub], p1[:, sub]], axis=0)
            v = jnp.concatenate([v_buf[k0, h], v_buf[v1, h]], axis=1)
            acc[b, h] = acc[b, h] * scale[:, sub] + dot(v, p)

    parts = [(stream, pair) for stream in range(2) for pair in range(HEADS // 2)]
    for part in parts:
        score(0, s_even, peak_even, *part)

    def two(i, carry):
        for part in parts:
            score(2 * i + 1, s_odd, peak_odd, *part)
            update(2 * i, s_even, peak_even, *part)
        for part in parts:
            score(2 * i + 2, s_even, peak_even, *part)
            update(2 * i + 1, s_odd, peak_odd, *part)
        return carry

    lax.fori_loop(0, table[base + 2 * slots] >> 1, two, 0)
    if last:
        acc, top = states[1]
        for b in range(blocks):
            stat_ref[b, 0:1, :] = top[b, 0:1, :]
            for h in range(HEADS):
                half_ref[b, h] = acc[b, h, :LANES, :].astype(BF)
                stat_ref[b, 1:2, h * LANES : (h + 1) * LANES] = acc[b, h, LANES : LANES + 1, :]


def attend(slabs, group, tables, wk, wv_t, queries, factor, state, last):
    table, slots, table_width = tables
    rows, width = slabs[0].shape
    blocks = rows // TILE
    n = len(slabs)
    key_blocks = n * blocks
    first = state is None
    state_shapes = [
        jax.ShapeDtypeStruct((blocks + 1, HEADS, AUG, TILE), F32),
        jax.ShapeDtypeStruct((blocks + 1, 8, HEADS * LANES), F32),
    ] * 2
    out_shape, scratch = list(state_shapes), []
    if last:
        scratch = [pltpu.VMEM(a.shape, a.dtype) for a in state_shapes[2:]]
        out_shape[2:] = [
            jax.ShapeDtypeStruct((blocks, HEADS, LANES, TILE), BF),
            jax.ShapeDtypeStruct((blocks, 8, HEADS * LANES), F32),
        ]
    operands = [table, *slabs, wk, wv_t, queries]
    in_specs = [whole(pltpu.SMEM)] + [whole()] * (n + 3)
    aliases = {}
    if not first:
        aliases = {len(operands) + i: i for i in range(2 if last else 4)}
        operands += list(state)
        in_specs += [whole()] * 4
    return pl.pallas_call(
        functools.partial(
            attend_kernel, n, group * table_width, slots, blocks, factor, first, last
        ),
        out_shape=out_shape,
        in_specs=in_specs,
        out_specs=[whole()] * 4,
        input_output_aliases=aliases,
        scratch_shapes=scratch
        + [
            pltpu.VMEM((key_blocks, TILE, width), BF),
            pltpu.VMEM((key_blocks + 1, HEADS, AUG, TILE), BF),
            pltpu.VMEM((2, HEADS // 2, 2, TILE, PAIR), F32),
            pltpu.VMEM((2, HEADS // 2, 2, TILE, PAIR), F32),
            pltpu.VMEM((2, 8, width), F32),
            pltpu.VMEM((2, 8, width), F32),
        ],
        compiler_params=pltpu.CompilerParams(vmem_limit_bytes=ATTEND_LIMIT << 20),
        cost_estimate=pl.CostEstimate(
            flops=n * 2_000_000_000, bytes_accessed=8 << 20, transcendentals=0
        ),
        name="attend",
    )(*operands)


def finish_kernel(
    factor,
    acc_ref,
    top_ref,
    half_ref,
    stat_ref,
    x_ref,
    wo_ref,
    wg_ref,
    wu_ref,
    wd_ref,
    out_ref,
    att,
):
    rows, _ = x_ref.shape
    for b in range(rows // TILE):
        for h in range(HEADS):
            cols = slice(h * LANES, (h + 1) * LANES)
            m1 = top_ref[b, 0:1, cols]
            m2 = stat_ref[b, 0:1, cols]
            m = jnp.maximum(m1, m2)
            a1 = jnp.exp2((m1 - m) * factor)
            a2 = jnp.exp2((m2 - m) * factor)
            den = acc_ref[b, h, LANES : LANES + 1, :] * a1 + stat_ref[b, 1:2, cols] * a2
            num = acc_ref[b, h, :LANES, :] * a1 + half_ref[b, h].astype(F32) * a2
            att[b * TILE : (b + 1) * TILE, cols] = (num / den).T.astype(BF)
    residual = x_ref[...].astype(F32) + dot(att[...], wo_ref[...])
    inverse = lax.rsqrt(jnp.mean(residual * residual, axis=-1, keepdims=True) + 1e-06)
    normed = (residual * inverse).astype(BF)
    total = residual
    ff = wg_ref.shape[1]
    for start in range(0, ff, 512):
        cols = slice(start, min(start + 512, ff))
        gate = dot(normed, wg_ref[:, cols])
        up = dot(normed, wu_ref[:, cols])
        hidden = (gate / (1.0 + jnp.exp(-gate)) * up).astype(BF)
        total = total + dot(hidden, wd_ref[cols, :])
    out_ref[...] = total.astype(BF)


def finish(mine, theirs, x, w_out, w_gate, w_up, w_down, factor):
    rows, width = x.shape
    ff = w_gate.shape[1]
    return pl.pallas_call(
        functools.partial(finish_kernel, factor),
        out_shape=jax.ShapeDtypeStruct(x.shape, BF),
        in_specs=[whole()] * 9,
        out_specs=whole(),
        scratch_shapes=[pltpu.VMEM((rows, width), BF)],
        compiler_params=pltpu.CompilerParams(vmem_limit_bytes=FINISH_LIMIT << 20),
        cost_estimate=pl.CostEstimate(
            flops=2 * rows * width * (width + 3 * ff), bytes_accessed=12 << 20, transcendentals=0
        ),
        name="finish",
    )(*mine, *theirs, x, w_out, w_gate, w_up, w_down)


def pairs(zones, devs, move):
    out = []
    for zone in range(zones):
        for dev in range(devs):
            to = move(zone, dev)
            if to is not None:
                out.append((zone * devs + dev, to[0] * devs + to[1]))
    return out


def send(x, zones, devs, move):
    return lax.ppermute(x, ("zone", "dev"), pairs(zones, devs, move))


def walks(zones, devs):
    return zones == 4 and devs == 8


def walk_plan(zone, dev):
    n, f = zone ^ 1, zone ^ 3
    return [
        [(zone, dev)],
        [(zone, dev ^ 2), (n, dev)],
        [(zone, dev ^ 4), (n, dev ^ 2), (f, dev)],
        [(zone, dev ^ 6), (n, dev ^ 4), (f, dev ^ 2)],
        [(n, dev ^ 6), (f, dev ^ 4), (f, dev ^ 6)],
    ]


def walk_links(x, zones, devs, work):
    go = functools.partial(send, zones=zones, devs=devs)
    near = lambda a: go(a, move=lambda z, d: (z ^ 1, d))
    relay = lambda a: go(a, move=lambda z, d: (z ^ 2, d))
    inner = lambda d: d // 2 in (1, 2)
    middle = lambda a: go(a, move=lambda z, d: (z, d ^ 6) if inner(d) else None)
    outer = lambda a: go(a, move=lambda z, d: (z, d ^ 2) if inner(d) else None)
    ends = lambda a: go(a, move=lambda z, d: (z, d ^ 6) if not inner(d) else None)

    a1 = go(x, move=lambda z, d: (z, d ^ 2))
    n0 = near(x)
    p2 = middle(x)
    work([x])
    p4 = outer(p2)
    n1 = near(a1)
    f0 = relay(n0)
    p3 = middle(a1)
    work([a1, n0])
    p5 = outer(p3)
    f1 = relay(n1)
    a2 = pick(p4, p3)
    n2 = near(a2)
    g_inner = middle(f0)
    work([a2, n1, f0])
    a3 = pick(p5, p2)
    n3 = near(a3)
    f2 = relay(n2)
    g_ends = ends(f0)
    work([a3, n2, f1])
    f3 = pick(g_ends, g_inner)
    work([n3, f2, f3])


def gather_plan(zone, dev, zones, devs):
    return [
        [(where, 2 * c + dev % 2) for c in range(start, min(start + 2, devs // 2))]
        for where in (zone, (zone - 1) % zones, (zone + 1) % zones)
        for start in range(0, devs // 2, 2)
    ]


def gather_zones(x, zones, devs, work):
    chips = devs // 2
    ahead = lax.ppermute(x, "zone", [(i, (i + 1) % zones) for i in range(zones)])
    behind = lax.ppermute(x, "zone", [((i + 1) % zones, i) for i in range(zones)])
    same_core = [[d for d in range(devs) if d % 2 == c] for c in range(2)]
    for slab in (x, ahead, behind):
        every = lax.all_gather(slab, "dev", axis=0, axis_index_groups=same_core)
        for start in range(0, chips, 2):
            work([every[c] for c in range(start, min(start + 2, chips))])


def body(
    node_features,
    neighbour_blocks,
    neighbour_count,
    tile_valid,
    w_query,
    w_key,
    w_value,
    w_out,
    w_gate,
    w_up,
    w_down,
):
    _, width = node_features.shape
    zones, devs = lax.axis_size("zone"), lax.axis_size("dev")
    factor = math.log2(math.e) / math.sqrt(width // HEADS)
    go = functools.partial(send, zones=zones, devs=devs)
    swap = lambda a: go(a, move=lambda z, d: (z, d ^ 1))

    partner = swap(node_features)
    listed = swap(neighbour_blocks)
    if walks(zones, devs):
        plan, run = walk_plan, walk_links
    else:
        plan, run = functools.partial(gather_plan, zones=zones, devs=devs), gather_zones
    sizes = [len(group) for group in plan(0, 0)]
    tables, queries, wv_t = prepare(
        plan,
        sizes,
        neighbour_count,
        tile_valid,
        neighbour_blocks,
        listed,
        node_features,
        partner,
        w_query,
        w_value,
    )
    state, turn = None, 0

    def work(slabs):
        nonlocal state, turn
        last = turn == len(sizes) - 1
        state = attend(slabs, turn, tables, w_key, wv_t, queries, factor, state, last)
        turn += 1

    run(node_features, zones, devs, work)
    theirs = [swap(state[2]), swap(state[3])]
    return finish(state[:2], theirs, node_features, w_out, w_gate, w_up, w_down, factor)


def solution(mesh):
    placed = (
        P(("zone", "dev"), None),
        P(("zone", "dev"), None),
        P(("zone", "dev")),
        P(),
        P(),
        P(),
        P(),
        P(),
        P(),
        P(),
        P(),
    )

    return jax.shard_map(
        body, mesh=mesh, in_specs=placed, out_specs=P(("zone", "dev"), None), check_vma=False
    )
```

```python
import functools
import math

import jax
import jax.numpy as jnp
from jax import lax
from jax.experimental import pallas as pl
from jax.experimental.pallas import tpu as pltpu
from jax.sharding import PartitionSpec as P


TILE = 128
HEADS = 4
LANES = 128
PAIR = 2 * LANES
AUG = LANES + 16
NEG = -1e30
ATTEND_LIMIT = 20
FINISH_LIMIT = 24
BF = jnp.bfloat16
F32 = jnp.float32


def dot(a, b):
    return jnp.dot(a, b, preferred_element_type=F32)


def dot_t(a, b):
    return lax.dot_general(a, b, (((1,), (1,)), ((), ())), preferred_element_type=F32)


def whole(memory_space=pltpu.VMEM):
    return pl.BlockSpec(memory_space=memory_space)


def fill_tables(groups, slots, width, blocks, count_ref, valid_ref, own_ref, partner_ref, out_ref, scratch):
    listed, member, flat, sem = scratch
    zone_blocks = blocks * lax.axis_size("dev")
    rows, slots_listed = own_ref.shape
    row = lax.broadcasted_iota(jnp.int32, (rows, slots_listed), 0)
    lane = lax.broadcasted_iota(jnp.int32, (rows, slots_listed), 1)
    count = jnp.zeros((rows, slots_listed), jnp.int32)
    for r in range(rows):
        count = jnp.where(row == r, count_ref[r], count)
    listed[:rows, :] = jnp.where(lane < count, own_ref[...], -1)
    listed[rows:, :] = jnp.where(lane < count, partner_ref[...], -1)
    every = listed[...]
    wide = lax.broadcasted_iota(jnp.int32, member.shape, 1)
    found = jnp.zeros(member.shape, jnp.int32)
    k = 0
    ids = []
    for group in groups:
        ids.append([])
        for z, d in group:
            for j in range(blocks):
                block = z * zone_blocks + d * blocks + j
                hit = jnp.max(jnp.where(every == block, 1, 0), axis=1, keepdims=True)
                found = jnp.where(wide == k, hit, found)
                ids[-1].append(block)
                k += 1
    member[...] = found
    copy = pltpu.make_async_copy(member, flat, sem)
    copy.start()
    copy.wait()
    base = 0
    for g, group in enumerate(ids):
        ends = []
        for stream in range(2):
            start = g * width + stream * slots
            pos = jnp.int32(start)
            for b in range(blocks):
                for j in range(len(group)):
                    out_ref[pos] = j + 256 * b
                    pos = pos + flat[stream * blocks + b, base + j]
                out_ref[pos] = out_ref[jnp.maximum(pos - 1, start)] + 65536
                pos = pos + ((pos - start) & 1)
            ends.append(pos - start)
        steps = jnp.maximum(ends[0], ends[1]) >> 1
        steps = steps + (steps & 1)
        for stream in range(2):

            def fill(i, carry, start=g * width + stream * slots):
                out_ref[start + 2 * i] = 256 * blocks
                out_ref[start + 2 * i + 1] = 256 * blocks + 65536
                return carry

            lax.fori_loop(ends[stream] >> 1, steps + 1, fill, 0)
        out_ref[g * width + 2 * slots] = steps
        for j, block in enumerate(group):
            out_ref[g * width + 2 * slots + 1 + j] = valid_ref[block]
        base += len(group)


def prepare_kernel(plan, blocks, slots, width, *refs):
    count_hbm, valid_hbm, own_list_hbm, partner_list_hbm, x_hbm, wq_hbm, wv_hbm, partner_ref = refs[:8]
    table_ref, out_ref, wv_t_ref = refs[8:11]
    count, valid, own_list, partner_list, x_ref, wq_ref, wv_ref = refs[11:18]
    scratch, sems = refs[18:22], refs[22]
    moves = (
        (count_hbm, count),
        (valid_hbm, valid),
        (own_list_hbm, own_list),
        (partner_list_hbm, partner_list),
        (wq_hbm, wq_ref),
        (x_hbm, x_ref),
        (wv_hbm, wv_ref),
    )
    loads = [pltpu.make_async_copy(a, b, sems.at[i]) for i, (a, b) in enumerate(moves)]
    for load in loads:
        load.start()
    for load in loads[:4]:
        load.wait()
    groups = plan(lax.axis_index("zone"), lax.axis_index("dev"))
    fill_tables(groups, slots, width, blocks, count, valid, own_list, partner_list, table_ref, scratch)
    for load in loads[4:]:
        load.wait()
    wv_t_ref[...] = wv_ref[...].T
    wq_t = wq_ref[...].T
    zero = jnp.zeros((LANES, TILE), BF)
    for half, ref in enumerate((x_ref, partner_ref)):
        q_t = dot_t(wq_t, ref[...]).astype(BF)
        for b in range(blocks):
            col = slice(b * TILE, (b + 1) * TILE)
            for pair in range(HEADS // 2):
                slot = out_ref.at[half * blocks + b, pair]
                slot[:LANES, :LANES] = q_t[pair * PAIR : pair * PAIR + LANES, col]
                slot[:LANES, LANES:] = zero
                slot[LANES:, :LANES] = zero
                slot[LANES:, LANES:] = q_t[pair * PAIR + LANES : (pair + 1) * PAIR, col]


def prepare(plan, sizes, counts, tile_valid, listed, partner_listed, x, partner, wq, wv):
    blocks = x.shape[0] // TILE
    slots = blocks * max(sizes) * blocks + 4
    width = 2 * slots + 1 + blocks * max(sizes)
    width += -width % LANES
    keys = sum(sizes) * blocks
    keys += -keys % LANES
    table, queries, wv_t = pl.pallas_call(
        functools.partial(prepare_kernel, plan, blocks, slots, width),
        out_shape=[
            jax.ShapeDtypeStruct((len(sizes) * width,), jnp.int32),
            jax.ShapeDtypeStruct((2 * blocks, HEADS // 2, PAIR, PAIR), BF),
            jax.ShapeDtypeStruct(wv.shape, BF),
        ],
        in_specs=[whole(pltpu.HBM)] * 3 + [whole(pl.ANY)] + [whole(pltpu.HBM)] * 3 + [whole()],
        out_specs=[whole(pltpu.SMEM), whole(), whole()],
        scratch_shapes=[
            pltpu.SMEM(counts.shape, jnp.int32),
            pltpu.SMEM(tile_valid.shape, jnp.int32),
            pltpu.VMEM(listed.shape, jnp.int32),
            pltpu.VMEM(listed.shape, jnp.int32),
            pltpu.VMEM(x.shape, BF),
            pltpu.VMEM(wq.shape, BF),
            pltpu.VMEM(wv.shape, BF),
            pltpu.VMEM((2 * blocks, listed.shape[1]), jnp.int32),
            pltpu.VMEM((2 * blocks, keys), jnp.int32),
            pltpu.SMEM((2 * blocks, keys), jnp.int32),
            pltpu.SemaphoreType.DMA,
            pltpu.SemaphoreType.DMA((7,)),
        ],
        compiler_params=pltpu.CompilerParams(vmem_limit_bytes=16 << 20),
        cost_estimate=pl.CostEstimate(
            flops=4 * x.shape[0] * x.shape[1] ** 2, bytes_accessed=4 << 20, transcendentals=0
        ),
        name="prepare",
    )(
        *[pltpu.with_memory_space_constraint(a, pltpu.HBM) for a in (counts, tile_valid, listed)],
        partner_listed,
        *[pltpu.with_memory_space_constraint(a, pltpu.HBM) for a in (x, wq, wv)],
        partner,
    )
    return (table, slots, width), queries, wv_t


def pick_kernel(edge_ref, inner_ref, out_ref):
    chip = lax.axis_index("dev") // 2
    at_edge = (chip == 0) | (chip == lax.axis_size("dev") // 2 - 1)

    @pl.when(at_edge)
    def _():
        out_ref[...] = edge_ref[...]

    @pl.when(jnp.logical_not(at_edge))
    def _():
        out_ref[...] = inner_ref[...]


def pick(at_edge, inner):
    return pl.pallas_call(
        pick_kernel,
        out_shape=jax.ShapeDtypeStruct(inner.shape, inner.dtype),
        in_specs=[whole()] * 2,
        out_specs=whole(),
        compiler_params=pltpu.CompilerParams(vmem_limit_bytes=8 << 20),
        cost_estimate=pl.CostEstimate(flops=0, bytes_accessed=1 << 20, transcendentals=0),
        name="pick",
    )(at_edge, inner)


def attend_kernel(n_slabs, base, slots, blocks, factor, first, last, *refs):
    table = refs[0]
    slabs = refs[1 : 1 + n_slabs]
    wk_ref, wv_t_ref, q_ref = refs[1 + n_slabs : 4 + n_slabs]
    rest = refs[4 + n_slabs :]
    olds, rest = ([], rest) if first else (rest[:4], rest[4:])
    outs, rest = rest[:4], rest[4:]
    if last:
        half_ref, stat_ref, rest = outs[2], outs[3], rest
        outs, rest = outs[:2] + rest[:2], rest[2:]
    states = ((outs[0], outs[1]), (outs[2], outs[3]))
    k_buf, v_buf, s_even, s_odd, peak_even, peak_odd = rest
    key_blocks = n_slabs * blocks
    if first:
        for acc, top in states:
            acc[...] = jnp.zeros_like(acc)
            top[...] = jnp.full_like(top, NEG)
    for old, out in zip(olds, outs):
        out[...] = old[...]
    v_buf[key_blocks] = jnp.zeros(v_buf.shape[1:], BF)

    def entry(stream, i):
        e0 = table[base + stream * slots + 2 * i]
        e1 = table[base + stream * slots + 2 * i + 1]
        k0, k1 = e0 & 255, e1 & 255
        return (e0 >> 8) & 255, k0, k1, jnp.where(e1 >= 65536, key_blocks, k1)

    for i, x in enumerate(slabs):
        row = lax.broadcasted_iota(jnp.int32, (TILE, x.shape[1]), 0)
        lane = lax.broadcasted_iota(jnp.int32, (AUG - LANES, TILE), 1)
        filled, zeroed = [], []
        for j in range(blocks):
            valid = table[base + 2 * slots + 1 + i * blocks + j]
            keep = jnp.where(row < valid, 1.0, 0.0).astype(BF)
            tile = x[j * TILE : (j + 1) * TILE, :]
            part = tile * keep
            zeroed.append(part)
            filled.append(part + tile[0:1, :] * (1 - keep))
            ones = jnp.where(lane < valid, 1.0, 0.0).astype(BF)
            for h in range(HEADS):
                v_buf[i * blocks + j, h, LANES:, :] = ones
        keys = dot(jnp.concatenate(filled, 0), wk_ref[...]).astype(BF)
        vals = dot_t(wv_t_ref[...], jnp.concatenate(zeroed, 0)).astype(BF)
        for j in range(blocks):
            k_buf[i * blocks + j] = keys[j * TILE : (j + 1) * TILE, :]
            for h in range(HEADS):
                v_buf[i * blocks + j, h, :LANES, :] = vals[
                    h * LANES : (h + 1) * LANES, j * TILE : (j + 1) * TILE
                ]

    def score(i, buf, peaks, stream, pair):
        b, k0, k1, _ = entry(stream, i)
        cols = slice(pair * PAIR, (pair + 1) * PAIR)
        q = q_ref[jnp.minimum(b, blocks - 1) + stream * blocks, pair]
        s0 = dot(k_buf[k0, :, cols], q)
        s1 = dot(k_buf[k1, :, cols], q)
        buf[stream, pair, 0] = s0
        buf[stream, pair, 1] = s1
        peaks[stream, 0:1, cols] = jnp.max(jnp.maximum(s0, s1), axis=0, keepdims=True)

    def update(i, buf, peaks, stream, pair):
        acc, top = states[stream]
        b, k0, _, v1 = entry(stream, i)
        cols = slice(pair * PAIR, (pair + 1) * PAIR)
        old = top[b, 0:1, cols]
        new = jnp.maximum(old, peaks[stream, 0:1, cols])
        scale = jnp.exp2((old - new) * factor)
        top[b, 0:1, cols] = new
        p0 = jnp.exp2((buf[stream, pair, 0] - new) * factor).astype(BF)
        p1 = jnp.exp2((buf[stream, pair, 1] - new) * factor).astype(BF)
        for side in range(2):
            h = pair * 2 + side
            sub = slice(side * LANES, (side + 1) * LANES)
            p = jnp.concatenate([p0[:, sub], p1[:, sub]], axis=0)
            v = jnp.concatenate([v_buf[k0, h], v_buf[v1, h]], axis=1)
            acc[b, h] = acc[b, h] * scale[:, sub] + dot(v, p)

    parts = [(stream, pair) for stream in range(2) for pair in range(HEADS // 2)]
    for part in parts:
        score(0, s_even, peak_even, *part)

    def two(i, carry):
        for part in parts:
            score(2 * i + 1, s_odd, peak_odd, *part)
            update(2 * i, s_even, peak_even, *part)
        for part in parts:
            score(2 * i + 2, s_even, peak_even, *part)
            update(2 * i + 1, s_odd, peak_odd, *part)
        return carry

    lax.fori_loop(0, table[base + 2 * slots] >> 1, two, 0)
    if last:
        acc, top = states[1]
        for b in range(blocks):
            stat_ref[b, 0:1, :] = top[b, 0:1, :]
            for h in range(HEADS):
                half_ref[b, h] = acc[b, h, :LANES, :].astype(BF)
                stat_ref[b, 1:2, h * LANES : (h + 1) * LANES] = acc[b, h, LANES : LANES + 1, :]


def attend(slabs, group, tables, wk, wv_t, queries, factor, state, last):
    table, slots, table_width = tables
    rows, width = slabs[0].shape
    blocks = rows // TILE
    n = len(slabs)
    key_blocks = n * blocks
    first = state is None
    state_shapes = [
        jax.ShapeDtypeStruct((blocks + 1, HEADS, AUG, TILE), F32),
        jax.ShapeDtypeStruct((blocks + 1, 8, HEADS * LANES), F32),
    ] * 2
    out_shape, scratch = list(state_shapes), []
    if last:
        scratch = [pltpu.VMEM(a.shape, a.dtype) for a in state_shapes[2:]]
        out_shape[2:] = [
            jax.ShapeDtypeStruct((blocks, HEADS, LANES, TILE), BF),
            jax.ShapeDtypeStruct((blocks, 8, HEADS * LANES), F32),
        ]
    operands = [table, *slabs, wk, wv_t, queries]
    in_specs = [whole(pltpu.SMEM)] + [whole()] * (n + 3)
    aliases = {}
    if not first:
        aliases = {len(operands) + i: i for i in range(2 if last else 4)}
        operands += list(state)
        in_specs += [whole()] * 4
    return pl.pallas_call(
        functools.partial(
            attend_kernel, n, group * table_width, slots, blocks, factor, first, last
        ),
        out_shape=out_shape,
        in_specs=in_specs,
        out_specs=[whole()] * 4,
        input_output_aliases=aliases,
        scratch_shapes=scratch
        + [
            pltpu.VMEM((key_blocks, TILE, width), BF),
            pltpu.VMEM((key_blocks + 1, HEADS, AUG, TILE), BF),
            pltpu.VMEM((2, HEADS // 2, 2, TILE, PAIR), F32),
            pltpu.VMEM((2, HEADS // 2, 2, TILE, PAIR), F32),
            pltpu.VMEM((2, 8, width), F32),
            pltpu.VMEM((2, 8, width), F32),
        ],
        compiler_params=pltpu.CompilerParams(vmem_limit_bytes=ATTEND_LIMIT << 20),
        cost_estimate=pl.CostEstimate(
            flops=n * 2_000_000_000, bytes_accessed=8 << 20, transcendentals=0
        ),
        name="attend",
    )(*operands)


def finish_kernel(
    factor,
    acc_ref,
    top_ref,
    half_ref,
    stat_ref,
    x_ref,
    wo_ref,
    wg_ref,
    wu_ref,
    wd_ref,
    out_ref,
    att,
):
    rows, _ = x_ref.shape
    for b in range(rows // TILE):
        for h in range(HEADS):
            cols = slice(h * LANES, (h + 1) * LANES)
            m1 = top_ref[b, 0:1, cols]
            m2 = stat_ref[b, 0:1, cols]
            m = jnp.maximum(m1, m2)
            a1 = jnp.exp2((m1 - m) * factor)
            a2 = jnp.exp2((m2 - m) * factor)
            den = acc_ref[b, h, LANES : LANES + 1, :] * a1 + stat_ref[b, 1:2, cols] * a2
            num = acc_ref[b, h, :LANES, :] * a1 + half_ref[b, h].astype(F32) * a2
            att[b * TILE : (b + 1) * TILE, cols] = (num / den).T.astype(BF)
    residual = x_ref[...].astype(F32) + dot(att[...], wo_ref[...])
    inverse = lax.rsqrt(jnp.mean(residual * residual, axis=-1, keepdims=True) + 1e-06)
    normed = (residual * inverse).astype(BF)
    total = residual
    ff = wg_ref.shape[1]
    for start in range(0, ff, 512):
        cols = slice(start, min(start + 512, ff))
        gate = dot(normed, wg_ref[:, cols])
        up = dot(normed, wu_ref[:, cols])
        hidden = (gate / (1.0 + jnp.exp(-gate)) * up).astype(BF)
        total = total + dot(hidden, wd_ref[cols, :])
    out_ref[...] = total.astype(BF)


def finish(mine, theirs, x, w_out, w_gate, w_up, w_down, factor):
    rows, width = x.shape
    ff = w_gate.shape[1]
    return pl.pallas_call(
        functools.partial(finish_kernel, factor),
        out_shape=jax.ShapeDtypeStruct(x.shape, BF),
        in_specs=[whole()] * 9,
        out_specs=whole(),
        scratch_shapes=[pltpu.VMEM((rows, width), BF)],
        compiler_params=pltpu.CompilerParams(vmem_limit_bytes=FINISH_LIMIT << 20),
        cost_estimate=pl.CostEstimate(
            flops=2 * rows * width * (width + 3 * ff), bytes_accessed=12 << 20, transcendentals=0
        ),
        name="finish",
    )(*mine, *theirs, x, w_out, w_gate, w_up, w_down)


def pairs(zones, devs, move):
    out = []
    for zone in range(zones):
        for dev in range(devs):
            to = move(zone, dev)
            if to is not None:
                out.append((zone * devs + dev, to[0] * devs + to[1]))
    return out


def send(x, zones, devs, move):
    return lax.ppermute(x, ("zone", "dev"), pairs(zones, devs, move))


def walks(zones, devs):
    return zones == 4 and devs == 8


def walk_plan(zone, dev):
    n, f = zone ^ 1, zone ^ 3
    return [
        [(zone, dev)],
        [(zone, dev ^ 2), (n, dev)],
        [(zone, dev ^ 4), (n, dev ^ 2), (f, dev)],
        [(zone, dev ^ 6), (n, dev ^ 4), (f, dev ^ 2)],
        [(n, dev ^ 6), (f, dev ^ 4)],
        [(f, dev ^ 6)],
    ]


def walk_links(x, zones, devs, work):
    go = functools.partial(send, zones=zones, devs=devs)
    near = lambda a: go(a, move=lambda z, d: (z ^ 1, d))
    relay = lambda a: go(a, move=lambda z, d: (z ^ 2, d))
    inner = lambda d: d // 2 in (1, 2)
    middle = lambda a: go(a, move=lambda z, d: (z, d ^ 6) if inner(d) else None)
    outer = lambda a: go(a, move=lambda z, d: (z, d ^ 2) if inner(d) else None)
    ends = lambda a: go(a, move=lambda z, d: (z, d ^ 6) if not inner(d) else None)

    a1 = go(x, move=lambda z, d: (z, d ^ 2))
    n0 = near(x)
    p2 = middle(x)
    work([x])
    p4 = outer(p2)
    n1 = near(a1)
    f0 = relay(n0)
    p3 = middle(a1)
    work([a1, n0])
    p5 = outer(p3)
    f1 = relay(n1)
    a2 = pick(p4, p3)
    n2 = near(a2)
    g_inner = middle(f0)
    work([a2, n1, f0])
    a3 = pick(p5, p2)
    n3 = near(a3)
    f2 = relay(n2)
    g_ends = ends(f0)
    work([a3, n2, f1])
    work([n3, f2])
    work([pick(g_ends, g_inner)])


def gather_plan(zone, dev, zones, devs):
    return [
        [(where, 2 * c + dev % 2) for c in range(start, min(start + 2, devs // 2))]
        for where in (zone, (zone - 1) % zones, (zone + 1) % zones)
        for start in range(0, devs // 2, 2)
    ]


def gather_zones(x, zones, devs, work):
    chips = devs // 2
    ahead = lax.ppermute(x, "zone", [(i, (i + 1) % zones) for i in range(zones)])
    behind = lax.ppermute(x, "zone", [((i + 1) % zones, i) for i in range(zones)])
    same_core = [[d for d in range(devs) if d % 2 == c] for c in range(2)]
    for slab in (x, ahead, behind):
        every = lax.all_gather(slab, "dev", axis=0, axis_index_groups=same_core)
        for start in range(0, chips, 2):
            work([every[c] for c in range(start, min(start + 2, chips))])


def body(
    node_features,
    neighbour_blocks,
    neighbour_count,
    tile_valid,
    w_query,
    w_key,
    w_value,
    w_out,
    w_gate,
    w_up,
    w_down,
):
    _, width = node_features.shape
    zones, devs = lax.axis_size("zone"), lax.axis_size("dev")
    factor = math.log2(math.e) / math.sqrt(width // HEADS)
    go = functools.partial(send, zones=zones, devs=devs)
    swap = lambda a: go(a, move=lambda z, d: (z, d ^ 1))

    partner = swap(node_features)
    listed = swap(neighbour_blocks)
    if walks(zones, devs):
        plan, run = walk_plan, walk_links
    else:
        plan, run = functools.partial(gather_plan, zones=zones, devs=devs), gather_zones
    sizes = [len(group) for group in plan(0, 0)]
    tables, queries, wv_t = prepare(
        plan,
        sizes,
        neighbour_count,
        tile_valid,
        neighbour_blocks,
        listed,
        node_features,
        partner,
        w_query,
        w_value,
    )
    state, turn = None, 0

    def work(slabs):
        nonlocal state, turn
        last = turn == len(sizes) - 1
        state = attend(slabs, turn, tables, w_key, wv_t, queries, factor, state, last)
        turn += 1

    run(node_features, zones, devs, work)
    theirs = [swap(state[2]), swap(state[3])]
    return finish(state[:2], theirs, node_features, w_out, w_gate, w_up, w_down, factor)


def solution(mesh):
    placed = (
        P(("zone", "dev"), None),
        P(("zone", "dev"), None),
        P(("zone", "dev")),
        P(),
        P(),
        P(),
        P(),
        P(),
        P(),
        P(),
        P(),
    )

    return jax.shard_map(
        body, mesh=mesh, in_specs=placed, out_specs=P(("zone", "dev"), None), check_vma=False
    )
```

```python
import functools
import math

import jax
import jax.numpy as jnp
from jax import lax
from jax.experimental import pallas as pl
from jax.experimental.pallas import tpu as pltpu
from jax.sharding import PartitionSpec as P


TILE = 128
HEADS = 4
LANES = 128
PAIR = 2 * LANES
AUG = LANES + 16
NEG = -1e30
ATTEND_LIMIT = 20
FINISH_LIMIT = 24
BF = jnp.bfloat16
F32 = jnp.float32


def dot(a, b):
    return jnp.dot(a, b, preferred_element_type=F32)


def dot_t(a, b):
    return lax.dot_general(a, b, (((1,), (1,)), ((), ())), preferred_element_type=F32)


def whole(memory_space=pltpu.VMEM):
    return pl.BlockSpec(memory_space=memory_space)


def fill_tables(groups, slots, width, blocks, count_ref, valid_ref, own_ref, partner_ref, out_ref, scratch):
    listed, member, flat, sem = scratch
    zone_blocks = blocks * lax.axis_size("dev")
    rows, slots_listed = own_ref.shape
    row = lax.broadcasted_iota(jnp.int32, (rows, slots_listed), 0)
    lane = lax.broadcasted_iota(jnp.int32, (rows, slots_listed), 1)
    count = jnp.zeros((rows, slots_listed), jnp.int32)
    for r in range(rows):
        count = jnp.where(row == r, count_ref[r], count)
    listed[:rows, :] = jnp.where(lane < count, own_ref[...], -1)
    listed[rows:, :] = jnp.where(lane < count, partner_ref[...], -1)
    every = listed[...]
    wide = lax.broadcasted_iota(jnp.int32, member.shape, 1)
    found = jnp.zeros(member.shape, jnp.int32)
    k = 0
    ids = []
    for group in groups:
        ids.append([])
        for z, d in group:
            for j in range(blocks):
                block = z * zone_blocks + d * blocks + j
                hit = jnp.max(jnp.where(every == block, 1, 0), axis=1, keepdims=True)
                found = jnp.where(wide == k, hit, found)
                ids[-1].append(block)
                k += 1
    member[...] = found
    copy = pltpu.make_async_copy(member, flat, sem)
    copy.start()
    copy.wait()
    base = 0
    for g, group in enumerate(ids):
        ends = []
        for stream in range(2):
            start = g * width + stream * slots
            pos = jnp.int32(start)
            for b in range(blocks):
                for j in range(len(group)):
                    out_ref[pos] = j + 256 * b
                    pos = pos + flat[stream * blocks + b, base + j]
                out_ref[pos] = out_ref[jnp.maximum(pos - 1, start)] + 65536
                pos = pos + ((pos - start) & 1)
            ends.append(pos - start)
        steps = jnp.maximum(ends[0], ends[1]) >> 1
        for stream in range(2):

            def fill(i, carry, start=g * width + stream * slots):
                out_ref[start + 2 * i] = 256 * blocks
                out_ref[start + 2 * i + 1] = 256 * blocks + 65536
                return carry

            lax.fori_loop(ends[stream] >> 1, steps + 1, fill, 0)
        out_ref[g * width + 2 * slots] = steps
        for j, block in enumerate(group):
            out_ref[g * width + 2 * slots + 1 + j] = valid_ref[block]
        base += len(group)


def prepare_kernel(plan, blocks, slots, width, *refs):
    count_hbm, valid_hbm, own_list_hbm, partner_list_hbm, x_hbm, wq_hbm, wv_hbm, partner_ref = refs[:8]
    table_ref, out_ref, wv_t_ref = refs[8:11]
    count, valid, own_list, partner_list, x_ref, wq_ref, wv_ref = refs[11:18]
    scratch, sems = refs[18:22], refs[22]
    moves = (
        (count_hbm, count),
        (valid_hbm, valid),
        (own_list_hbm, own_list),
        (partner_list_hbm, partner_list),
        (wq_hbm, wq_ref),
        (x_hbm, x_ref),
        (wv_hbm, wv_ref),
    )
    loads = [pltpu.make_async_copy(a, b, sems.at[i]) for i, (a, b) in enumerate(moves)]
    for load in loads:
        load.start()
    for load in loads[:4]:
        load.wait()
    groups = plan(lax.axis_index("zone"), lax.axis_index("dev"))
    fill_tables(groups, slots, width, blocks, count, valid, own_list, partner_list, table_ref, scratch)
    for load in loads[4:]:
        load.wait()
    wv_t_ref[...] = wv_ref[...].T
    wq_t = wq_ref[...].T
    zero = jnp.zeros((LANES, TILE), BF)
    for half, ref in enumerate((x_ref, partner_ref)):
        q_t = dot_t(wq_t, ref[...]).astype(BF)
        for b in range(blocks):
            col = slice(b * TILE, (b + 1) * TILE)
            for pair in range(HEADS // 2):
                slot = out_ref.at[half * blocks + b, pair]
                slot[:LANES, :LANES] = q_t[pair * PAIR : pair * PAIR + LANES, col]
                slot[:LANES, LANES:] = zero
                slot[LANES:, :LANES] = zero
                slot[LANES:, LANES:] = q_t[pair * PAIR + LANES : (pair + 1) * PAIR, col]


def prepare(plan, sizes, counts, tile_valid, listed, partner_listed, x, partner, wq, wv):
    blocks = x.shape[0] // TILE
    slots = blocks * max(sizes) * blocks + 4
    width = 2 * slots + 1 + blocks * max(sizes)
    width += -width % LANES
    keys = sum(sizes) * blocks
    keys += -keys % LANES
    table, queries, wv_t = pl.pallas_call(
        functools.partial(prepare_kernel, plan, blocks, slots, width),
        out_shape=[
            jax.ShapeDtypeStruct((len(sizes) * width,), jnp.int32),
            jax.ShapeDtypeStruct((2 * blocks, HEADS // 2, PAIR, PAIR), BF),
            jax.ShapeDtypeStruct(wv.shape, BF),
        ],
        in_specs=[whole(pltpu.HBM)] * 3 + [whole(pl.ANY)] + [whole(pltpu.HBM)] * 3 + [whole()],
        out_specs=[whole(pltpu.SMEM), whole(), whole()],
        scratch_shapes=[
            pltpu.SMEM(counts.shape, jnp.int32),
            pltpu.SMEM(tile_valid.shape, jnp.int32),
            pltpu.VMEM(listed.shape, jnp.int32),
            pltpu.VMEM(listed.shape, jnp.int32),
            pltpu.VMEM(x.shape, BF),
            pltpu.VMEM(wq.shape, BF),
            pltpu.VMEM(wv.shape, BF),
            pltpu.VMEM((2 * blocks, listed.shape[1]), jnp.int32),
            pltpu.VMEM((2 * blocks, keys), jnp.int32),
            pltpu.SMEM((2 * blocks, keys), jnp.int32),
            pltpu.SemaphoreType.DMA,
            pltpu.SemaphoreType.DMA((7,)),
        ],
        compiler_params=pltpu.CompilerParams(vmem_limit_bytes=16 << 20),
        cost_estimate=pl.CostEstimate(
            flops=4 * x.shape[0] * x.shape[1] ** 2, bytes_accessed=4 << 20, transcendentals=0
        ),
        name="prepare",
    )(
        *[pltpu.with_memory_space_constraint(a, pltpu.HBM) for a in (counts, tile_valid, listed)],
        partner_listed,
        *[pltpu.with_memory_space_constraint(a, pltpu.HBM) for a in (x, wq, wv)],
        partner,
    )
    return (table, slots, width), queries, wv_t


def pick_kernel(edge_ref, inner_ref, out_ref):
    chip = lax.axis_index("dev") // 2
    at_edge = (chip == 0) | (chip == lax.axis_size("dev") // 2 - 1)

    @pl.when(at_edge)
    def _():
        out_ref[...] = edge_ref[...]

    @pl.when(jnp.logical_not(at_edge))
    def _():
        out_ref[...] = inner_ref[...]


def pick(at_edge, inner):
    return pl.pallas_call(
        pick_kernel,
        out_shape=jax.ShapeDtypeStruct(inner.shape, inner.dtype),
        in_specs=[whole()] * 2,
        out_specs=whole(),
        compiler_params=pltpu.CompilerParams(vmem_limit_bytes=8 << 20),
        cost_estimate=pl.CostEstimate(flops=0, bytes_accessed=1 << 20, transcendentals=0),
        name="pick",
    )(at_edge, inner)


def attend_kernel(n_slabs, base, slots, blocks, factor, first, last, *refs):
    table = refs[0]
    slabs = refs[1 : 1 + n_slabs]
    wk_ref, wv_t_ref, q_ref = refs[1 + n_slabs : 4 + n_slabs]
    rest = refs[4 + n_slabs :]
    olds, rest = ([], rest) if first else (rest[:4], rest[4:])
    outs, rest = rest[:4], rest[4:]
    if last:
        half_ref, stat_ref, rest = outs[2], outs[3], rest
        outs, rest = outs[:2] + rest[:2], rest[2:]
    states = ((outs[0], outs[1]), (outs[2], outs[3]))
    k_buf, v_buf, s_even, s_odd, peak_even, peak_odd = rest
    key_blocks = n_slabs * blocks
    if first:
        for acc, top in states:
            acc[...] = jnp.zeros_like(acc)
            top[...] = jnp.full_like(top, NEG)
    chunks = [
        (old, out, j) for old, out in zip(olds, outs) for j in range(old.shape[0])
    ]

    def carry_over(i):
        for old, out, j in chunks[i :: 2 * n_slabs]:
            out[j] = old[j]

    v_buf[key_blocks] = jnp.zeros(v_buf.shape[1:], BF)

    def entry(stream, i):
        e0 = table[base + stream * slots + 2 * i]
        e1 = table[base + stream * slots + 2 * i + 1]
        k0, k1 = e0 & 255, e1 & 255
        return (e0 >> 8) & 255, k0, k1, jnp.where(e1 >= 65536, key_blocks, k1)

    for i, x in enumerate(slabs):
        row = lax.broadcasted_iota(jnp.int32, (TILE, x.shape[1]), 0)
        lane = lax.broadcasted_iota(jnp.int32, (AUG - LANES, TILE), 1)
        filled, zeroed = [], []
        for j in range(blocks):
            valid = table[base + 2 * slots + 1 + i * blocks + j]
            keep = jnp.where(row < valid, 1.0, 0.0).astype(BF)
            tile = x[j * TILE : (j + 1) * TILE, :]
            part = tile * keep
            zeroed.append(part)
            filled.append(part + tile[0:1, :] * (1 - keep))
            ones = jnp.where(lane < valid, 1.0, 0.0).astype(BF)
            for h in range(HEADS):
                v_buf[i * blocks + j, h, LANES:, :] = ones
        keys = dot(jnp.concatenate(filled, 0), wk_ref[...]).astype(BF)
        carry_over(2 * i)
        vals = dot_t(wv_t_ref[...], jnp.concatenate(zeroed, 0)).astype(BF)
        carry_over(2 * i + 1)
        for j in range(blocks):
            k_buf[i * blocks + j] = keys[j * TILE : (j + 1) * TILE, :]
            for h in range(HEADS):
                v_buf[i * blocks + j, h, :LANES, :] = vals[
                    h * LANES : (h + 1) * LANES, j * TILE : (j + 1) * TILE
                ]

    def score(i, buf, peaks, stream, pair):
        b, k0, k1, _ = entry(stream, i)
        cols = slice(pair * PAIR, (pair + 1) * PAIR)
        q = q_ref[jnp.minimum(b, blocks - 1) + stream * blocks, pair]
        s0 = dot(k_buf[k0, :, cols], q)
        s1 = dot(k_buf[k1, :, cols], q)
        buf[stream, pair, 0] = s0
        buf[stream, pair, 1] = s1
        peaks[stream, 0:1, cols] = jnp.max(jnp.maximum(s0, s1), axis=0, keepdims=True)

    def update(i, buf, peaks, stream, pair):
        acc, top = states[stream]
        b, k0, _, v1 = entry(stream, i)
        cols = slice(pair * PAIR, (pair + 1) * PAIR)
        old = top[b, 0:1, cols]
        new = jnp.maximum(old, peaks[stream, 0:1, cols])
        scale = jnp.exp2((old - new) * factor)
        top[b, 0:1, cols] = new
        p0 = jnp.exp2((buf[stream, pair, 0] - new) * factor).astype(BF)
        p1 = jnp.exp2((buf[stream, pair, 1] - new) * factor).astype(BF)
        for side in range(2):
            h = pair * 2 + side
            sub = slice(side * LANES, (side + 1) * LANES)
            p = jnp.concatenate([p0[:, sub], p1[:, sub]], axis=0)
            v = jnp.concatenate([v_buf[k0, h], v_buf[v1, h]], axis=1)
            acc[b, h] = acc[b, h] * scale[:, sub] + dot(v, p)

    parts = [(stream, pair) for stream in range(2) for pair in range(HEADS // 2)]
    for part in parts:
        score(0, s_even, peak_even, *part)

    def two(i, carry):
        for before, part in zip(parts[-1:] + parts[:-1], parts):
            score(2 * i + 1, s_odd, peak_odd, *before)
            update(2 * i, s_even, peak_even, *part)
        for before, part in zip(parts[-1:] + parts[:-1], parts):
            score(2 * i + 2, s_even, peak_even, *before)
            update(2 * i + 1, s_odd, peak_odd, *part)
        return carry

    steps = table[base + 2 * slots]
    lax.fori_loop(0, steps >> 1, two, 0)

    @pl.when((steps & 1) == 1)
    def _():
        for part in parts:
            update(steps - 1, s_even, peak_even, *part)

    if last:
        acc, top = states[1]
        for b in range(blocks):
            stat_ref[b, 0:1, :] = top[b, 0:1, :]
            for h in range(HEADS):
                half_ref[b, h] = acc[b, h, :LANES, :].astype(BF)
                stat_ref[b, 1:2, h * LANES : (h + 1) * LANES] = acc[b, h, LANES : LANES + 1, :]


def attend(slabs, group, tables, wk, wv_t, queries, factor, state, last):
    table, slots, table_width = tables
    rows, width = slabs[0].shape
    blocks = rows // TILE
    n = len(slabs)
    key_blocks = n * blocks
    first = state is None
    state_shapes = [
        jax.ShapeDtypeStruct((blocks + 1, HEADS, AUG, TILE), F32),
        jax.ShapeDtypeStruct((blocks + 1, 8, HEADS * LANES), F32),
    ] * 2
    out_shape, scratch = list(state_shapes), []
    if last:
        scratch = [pltpu.VMEM(a.shape, a.dtype) for a in state_shapes[2:]]
        out_shape[2:] = [
            jax.ShapeDtypeStruct((blocks, HEADS, LANES, TILE), BF),
            jax.ShapeDtypeStruct((blocks, 8, HEADS * LANES), F32),
        ]
    operands = [table, *slabs, wk, wv_t, queries]
    in_specs = [whole(pltpu.SMEM)] + [whole()] * (n + 3)
    aliases = {}
    if not first:
        aliases = {len(operands) + i: i for i in range(2 if last else 4)}
        operands += list(state)
        in_specs += [whole()] * 4
    return pl.pallas_call(
        functools.partial(
            attend_kernel, n, group * table_width, slots, blocks, factor, first, last
        ),
        out_shape=out_shape,
        in_specs=in_specs,
        out_specs=[whole()] * 4,
        input_output_aliases=aliases,
        scratch_shapes=scratch
        + [
            pltpu.VMEM((key_blocks, TILE, width), BF),
            pltpu.VMEM((key_blocks + 1, HEADS, AUG, TILE), BF),
            pltpu.VMEM((2, HEADS // 2, 2, TILE, PAIR), F32),
            pltpu.VMEM((2, HEADS // 2, 2, TILE, PAIR), F32),
            pltpu.VMEM((2, 8, width), F32),
            pltpu.VMEM((2, 8, width), F32),
        ],
        compiler_params=pltpu.CompilerParams(vmem_limit_bytes=ATTEND_LIMIT << 20),
        cost_estimate=pl.CostEstimate(
            flops=n * 2_000_000_000, bytes_accessed=8 << 20, transcendentals=0
        ),
        name="attend",
    )(*operands)


def finish_kernel(
    factor,
    acc_ref,
    top_ref,
    half_ref,
    stat_ref,
    x_ref,
    wo_ref,
    wg_ref,
    wu_ref,
    wd_ref,
    out_ref,
    att,
):
    rows, _ = x_ref.shape
    for b in range(rows // TILE):
        for h in range(HEADS):
            cols = slice(h * LANES, (h + 1) * LANES)
            m1 = top_ref[b, 0:1, cols]
            m2 = stat_ref[b, 0:1, cols]
            m = jnp.maximum(m1, m2)
            a1 = jnp.exp2((m1 - m) * factor)
            a2 = jnp.exp2((m2 - m) * factor)
            den = acc_ref[b, h, LANES : LANES + 1, :] * a1 + stat_ref[b, 1:2, cols] * a2
            num = acc_ref[b, h, :LANES, :] * a1 + half_ref[b, h].astype(F32) * a2
            att[b * TILE : (b + 1) * TILE, cols] = (num / den).T.astype(BF)
    residual = x_ref[...].astype(F32) + dot(att[...], wo_ref[...])
    inverse = lax.rsqrt(jnp.mean(residual * residual, axis=-1, keepdims=True) + 1e-06)
    normed = (residual * inverse).astype(BF)
    total = residual
    ff = wg_ref.shape[1]
    for start in range(0, ff, 512):
        cols = slice(start, min(start + 512, ff))
        gate = dot(normed, wg_ref[:, cols])
        up = dot(normed, wu_ref[:, cols])
        hidden = (gate / (1.0 + jnp.exp(-gate)) * up).astype(BF)
        total = total + dot(hidden, wd_ref[cols, :])
    out_ref[...] = total.astype(BF)


def finish(mine, theirs, x, w_out, w_gate, w_up, w_down, factor):
    rows, width = x.shape
    ff = w_gate.shape[1]
    return pl.pallas_call(
        functools.partial(finish_kernel, factor),
        out_shape=jax.ShapeDtypeStruct(x.shape, BF),
        in_specs=[whole()] * 9,
        out_specs=whole(),
        scratch_shapes=[pltpu.VMEM((rows, width), BF)],
        compiler_params=pltpu.CompilerParams(vmem_limit_bytes=FINISH_LIMIT << 20),
        cost_estimate=pl.CostEstimate(
            flops=2 * rows * width * (width + 3 * ff), bytes_accessed=12 << 20, transcendentals=0
        ),
        name="finish",
    )(*mine, *theirs, x, w_out, w_gate, w_up, w_down)


def pairs(zones, devs, move):
    out = []
    for zone in range(zones):
        for dev in range(devs):
            to = move(zone, dev)
            if to is not None:
                out.append((zone * devs + dev, to[0] * devs + to[1]))
    return out


def send(x, zones, devs, move):
    return lax.ppermute(x, ("zone", "dev"), pairs(zones, devs, move))


def walks(zones, devs):
    return zones == 4 and devs == 8


def walk_plan(zone, dev):
    n, f = zone ^ 1, zone ^ 3
    return [
        [(zone, dev), (zone, dev ^ 2), (n, dev)],
        [(zone, dev ^ 4), (n, dev ^ 2), (f, dev)],
        [(zone, dev ^ 6), (n, dev ^ 4), (f, dev ^ 2)],
        [(n, dev ^ 6), (f, dev ^ 4)],
        [(f, dev ^ 6)],
    ]


def walk_links(x, zones, devs, work):
    go = functools.partial(send, zones=zones, devs=devs)
    near = lambda a: go(a, move=lambda z, d: (z ^ 1, d))
    relay = lambda a: go(a, move=lambda z, d: (z ^ 2, d))
    inner = lambda d: d // 2 in (1, 2)
    middle = lambda a: go(a, move=lambda z, d: (z, d ^ 6) if inner(d) else None)
    outer = lambda a: go(a, move=lambda z, d: (z, d ^ 2) if inner(d) else None)
    ends = lambda a: go(a, move=lambda z, d: (z, d ^ 6) if not inner(d) else None)

    a1 = go(x, move=lambda z, d: (z, d ^ 2))
    n0 = near(x)
    p2 = middle(x)
    p4 = outer(p2)
    n1 = near(a1)
    f0 = relay(n0)
    p3 = middle(a1)
    work([x, a1, n0])
    p5 = outer(p3)
    f1 = relay(n1)
    a2 = pick(p4, p3)
    n2 = near(a2)
    g_inner = middle(f0)
    work([a2, n1, f0])
    a3 = pick(p5, p2)
    n3 = near(a3)
    f2 = relay(n2)
    g_ends = ends(f0)
    work([a3, n2, f1])
    work([n3, f2])
    work([pick(g_ends, g_inner)])


def gather_plan(zone, dev, zones, devs):
    return [
        [(where, 2 * c + dev % 2) for c in range(start, min(start + 2, devs // 2))]
        for where in (zone, (zone - 1) % zones, (zone + 1) % zones)
        for start in range(0, devs // 2, 2)
    ]


def gather_zones(x, zones, devs, work):
    chips = devs // 2
    ahead = lax.ppermute(x, "zone", [(i, (i + 1) % zones) for i in range(zones)])
    behind = lax.ppermute(x, "zone", [((i + 1) % zones, i) for i in range(zones)])
    same_core = [[d for d in range(devs) if d % 2 == c] for c in range(2)]
    for slab in (x, ahead, behind):
        every = lax.all_gather(slab, "dev", axis=0, axis_index_groups=same_core)
        for start in range(0, chips, 2):
            work([every[c] for c in range(start, min(start + 2, chips))])


def body(
    node_features,
    neighbour_blocks,
    neighbour_count,
    tile_valid,
    w_query,
    w_key,
    w_value,
    w_out,
    w_gate,
    w_up,
    w_down,
):
    _, width = node_features.shape
    zones, devs = lax.axis_size("zone"), lax.axis_size("dev")
    factor = math.log2(math.e) / math.sqrt(width // HEADS)
    go = functools.partial(send, zones=zones, devs=devs)
    swap = lambda a: go(a, move=lambda z, d: (z, d ^ 1))

    partner = swap(node_features)
    listed = swap(neighbour_blocks)
    if walks(zones, devs):
        plan, run = walk_plan, walk_links
    else:
        plan, run = functools.partial(gather_plan, zones=zones, devs=devs), gather_zones
    sizes = [len(group) for group in plan(0, 0)]
    tables, queries, wv_t = prepare(
        plan,
        sizes,
        neighbour_count,
        tile_valid,
        neighbour_blocks,
        listed,
        node_features,
        partner,
        w_query,
        w_value,
    )
    state, turn = None, 0

    def work(slabs):
        nonlocal state, turn
        last = turn == len(sizes) - 1
        state = attend(slabs, turn, tables, w_key, wv_t, queries, factor, state, last)
        turn += 1

    run(node_features, zones, devs, work)
    theirs = [swap(state[2]), swap(state[3])]
    return finish(state[:2], theirs, node_features, w_out, w_gate, w_up, w_down, factor)


def solution(mesh):
    placed = (
        P(("zone", "dev"), None),
        P(("zone", "dev"), None),
        P(("zone", "dev")),
        P(),
        P(),
        P(),
        P(),
        P(),
        P(),
        P(),
        P(),
    )

    return jax.shard_map(
        body, mesh=mesh, in_specs=placed, out_specs=P(("zone", "dev"), None), check_vma=False
    )
```

```python
import functools
import math

import jax
import jax.numpy as jnp
from jax import lax
from jax.experimental import pallas as pl
from jax.experimental.pallas import tpu as pltpu
from jax.sharding import PartitionSpec as P


TILE = 128
HEADS = 4
LANES = 128
PAIR = 2 * LANES
AUG = LANES + 16
NEG = -1e30
ATTEND_LIMIT = 20
FINISH_LIMIT = 24
BF = jnp.bfloat16
F32 = jnp.float32


def dot(a, b):
    return jnp.dot(a, b, preferred_element_type=F32)


def dot_t(a, b):
    return lax.dot_general(a, b, (((1,), (1,)), ((), ())), preferred_element_type=F32)


def whole(memory_space=pltpu.VMEM):
    return pl.BlockSpec(memory_space=memory_space)


def fill_tables(groups, slots, width, blocks, count_ref, valid_ref, own_ref, partner_ref, out_ref, scratch):
    listed, member, flat, sem = scratch
    zone_blocks = blocks * lax.axis_size("dev")
    rows, slots_listed = own_ref.shape
    row = lax.broadcasted_iota(jnp.int32, (rows, slots_listed), 0)
    lane = lax.broadcasted_iota(jnp.int32, (rows, slots_listed), 1)
    count = jnp.zeros((rows, slots_listed), jnp.int32)
    for r in range(rows):
        count = jnp.where(row == r, count_ref[r], count)
    listed[:rows, :] = jnp.where(lane < count, own_ref[...], -1)
    listed[rows:, :] = jnp.where(lane < count, partner_ref[...], -1)
    every = listed[...]
    wide = lax.broadcasted_iota(jnp.int32, member.shape, 1)
    found = jnp.zeros(member.shape, jnp.int32)
    k = 0
    ids = []
    for group in groups:
        ids.append([])
        for z, d in group:
            for j in range(blocks):
                block = z * zone_blocks + d * blocks + j
                hit = jnp.max(jnp.where(every == block, 1, 0), axis=1, keepdims=True)
                found = jnp.where(wide == k, hit, found)
                ids[-1].append(block)
                k += 1
    member[...] = found
    copy = pltpu.make_async_copy(member, flat, sem)
    copy.start()
    copy.wait()
    base = 0
    for g, group in enumerate(ids):
        start = g * width
        pos = jnp.int32(start)
        for b in range(2 * blocks):
            for j in range(len(group)):
                out_ref[pos] = j + 256 * b
                pos = pos + flat[b, base + j]
            out_ref[pos] = out_ref[jnp.maximum(pos - 1, start)] + 65536
            pos = pos + ((pos - start) & 1)
        pairs_listed = (pos - start) >> 1
        steps = (pairs_listed + 1) >> 1

        def fill(i, carry, start=start):
            out_ref[start + 2 * i] = 256 * 2 * blocks
            out_ref[start + 2 * i + 1] = 256 * 2 * blocks + 65536
            return carry

        lax.fori_loop(pairs_listed, 2 * steps + 2, fill, 0)
        out_ref[start + slots] = steps
        for j, block in enumerate(group):
            out_ref[start + slots + 1 + j] = valid_ref[block]
        base += len(group)


def prepare_kernel(plan, blocks, slots, width, *refs):
    count_hbm, valid_hbm, own_list_hbm, partner_list_hbm = refs[:4]
    x_hbm, wq_hbm, wv_hbm, wk_hbm, partner_ref = refs[4:9]
    table_ref, out_ref, wv_t_ref, x_ref, wk_ref = refs[9:14]
    count, valid, own_list, partner_list, wq_ref, wv_ref = refs[14:20]
    scratch, sems = refs[20:24], refs[24]
    moves = (
        (count_hbm, count),
        (valid_hbm, valid),
        (own_list_hbm, own_list),
        (partner_list_hbm, partner_list),
        (wq_hbm, wq_ref),
        (x_hbm, x_ref),
        (wv_hbm, wv_ref),
        (wk_hbm, wk_ref),
    )
    loads = [pltpu.make_async_copy(a, b, sems.at[i]) for i, (a, b) in enumerate(moves)]
    for load in loads:
        load.start()
    for load in loads[:4]:
        load.wait()
    groups = plan(lax.axis_index("zone"), lax.axis_index("dev"))
    fill_tables(groups, slots, width, blocks, count, valid, own_list, partner_list, table_ref, scratch)
    for load in loads[4:]:
        load.wait()
    wv_t_ref[...] = wv_ref[...].T
    wq_t = wq_ref[...].T
    zero = jnp.zeros((LANES, TILE), BF)
    for half, ref in enumerate((x_ref, partner_ref)):
        q_t = dot_t(wq_t, ref[...]).astype(BF)
        for b in range(blocks):
            col = slice(b * TILE, (b + 1) * TILE)
            for pair in range(HEADS // 2):
                slot = out_ref.at[half * blocks + b, pair]
                slot[:LANES, :LANES] = q_t[pair * PAIR : pair * PAIR + LANES, col]
                slot[:LANES, LANES:] = zero
                slot[LANES:, :LANES] = zero
                slot[LANES:, LANES:] = q_t[pair * PAIR + LANES : (pair + 1) * PAIR, col]


def prepare(plan, sizes, counts, tile_valid, listed, partner_listed, x, partner, wq, wv, wk):
    blocks = x.shape[0] // TILE
    slots = 2 * blocks * max(sizes) * blocks + 8
    width = slots + 1 + blocks * max(sizes)
    width += -width % LANES
    keys = sum(sizes) * blocks
    keys += -keys % LANES
    table, *local = pl.pallas_call(
        functools.partial(prepare_kernel, plan, blocks, slots, width),
        out_shape=[
            jax.ShapeDtypeStruct((len(sizes) * width,), jnp.int32),
            jax.ShapeDtypeStruct((2 * blocks, HEADS // 2, PAIR, PAIR), BF),
            jax.ShapeDtypeStruct(wv.shape, BF),
            jax.ShapeDtypeStruct(x.shape, BF),
            jax.ShapeDtypeStruct(wk.shape, BF),
        ],
        in_specs=[whole(pltpu.HBM)] * 3 + [whole(pl.ANY)] + [whole(pltpu.HBM)] * 4 + [whole()],
        out_specs=[whole(pltpu.SMEM)] + [whole()] * 4,
        scratch_shapes=[
            pltpu.SMEM(counts.shape, jnp.int32),
            pltpu.SMEM(tile_valid.shape, jnp.int32),
            pltpu.VMEM(listed.shape, jnp.int32),
            pltpu.VMEM(listed.shape, jnp.int32),
            pltpu.VMEM(wq.shape, BF),
            pltpu.VMEM(wv.shape, BF),
            pltpu.VMEM((2 * blocks, listed.shape[1]), jnp.int32),
            pltpu.VMEM((2 * blocks, keys), jnp.int32),
            pltpu.SMEM((2 * blocks, keys), jnp.int32),
            pltpu.SemaphoreType.DMA,
            pltpu.SemaphoreType.DMA((8,)),
        ],
        compiler_params=pltpu.CompilerParams(vmem_limit_bytes=16 << 20),
        cost_estimate=pl.CostEstimate(
            flops=4 * x.shape[0] * x.shape[1] ** 2, bytes_accessed=4 << 20, transcendentals=0
        ),
        name="prepare",
    )(
        *[pltpu.with_memory_space_constraint(a, pltpu.HBM) for a in (counts, tile_valid, listed)],
        partner_listed,
        *[pltpu.with_memory_space_constraint(a, pltpu.HBM) for a in (x, wq, wv, wk)],
        partner,
    )
    return (table, slots, width), *local


def pick_kernel(edge_ref, inner_ref, out_ref):
    chip = lax.axis_index("dev") // 2
    at_edge = (chip == 0) | (chip == lax.axis_size("dev") // 2 - 1)

    @pl.when(at_edge)
    def _():
        out_ref[...] = edge_ref[...]

    @pl.when(jnp.logical_not(at_edge))
    def _():
        out_ref[...] = inner_ref[...]


def pick(at_edge, inner):
    return pl.pallas_call(
        pick_kernel,
        out_shape=jax.ShapeDtypeStruct(inner.shape, inner.dtype),
        in_specs=[whole()] * 2,
        out_specs=whole(),
        compiler_params=pltpu.CompilerParams(vmem_limit_bytes=8 << 20),
        cost_estimate=pl.CostEstimate(flops=0, bytes_accessed=1 << 20, transcendentals=0),
        name="pick",
    )(at_edge, inner)


def attend_kernel(n_slabs, base, slots, blocks, factor, first, last, *refs):
    table = refs[0]
    slabs = refs[1 : 1 + n_slabs]
    wk_ref, wv_t_ref, q_ref = refs[1 + n_slabs : 4 + n_slabs]
    rest = refs[4 + n_slabs :]
    olds, rest = ([], rest) if first else (rest[:2], rest[2:])
    outs, rest = rest[:2], rest[2:]
    if last:
        half_ref, stat_ref, rest = rest[0], rest[1], rest[2:]
    acc, top = outs
    k_buf, v_buf, s_even, s_odd, peak_even, peak_odd = rest
    key_blocks = n_slabs * blocks
    if first:
        acc[...] = jnp.zeros_like(acc)
        top[...] = jnp.full_like(top, NEG)
    chunks = [
        (old, out, j) for old, out in zip(olds, outs) for j in range(old.shape[0])
    ]

    def carry_over(i):
        for old, out, j in chunks[i :: 2 * n_slabs]:
            out[j] = old[j]

    v_buf[key_blocks] = jnp.zeros(v_buf.shape[1:], BF)

    def entry(lane, i):
        e0 = table[base + 4 * i + 2 * lane]
        e1 = table[base + 4 * i + 2 * lane + 1]
        k0, k1 = e0 & 255, e1 & 255
        return (e0 >> 8) & 255, k0, k1, jnp.where(e1 >= 65536, key_blocks, k1)

    for i, x in enumerate(slabs):
        row = lax.broadcasted_iota(jnp.int32, (TILE, x.shape[1]), 0)
        lane = lax.broadcasted_iota(jnp.int32, (AUG - LANES, TILE), 1)
        filled, zeroed = [], []
        for j in range(blocks):
            valid = table[base + slots + 1 + i * blocks + j]
            keep = jnp.where(row < valid, 1.0, 0.0).astype(BF)
            tile = x[j * TILE : (j + 1) * TILE, :]
            part = tile * keep
            zeroed.append(part)
            filled.append(part + tile[0:1, :] * (1 - keep))
            ones = jnp.where(lane < valid, 1.0, 0.0).astype(BF)
            for h in range(HEADS):
                v_buf[i * blocks + j, h, LANES:, :] = ones
        keys = dot(jnp.concatenate(filled, 0), wk_ref[...]).astype(BF)
        carry_over(2 * i)
        vals = dot_t(wv_t_ref[...], jnp.concatenate(zeroed, 0)).astype(BF)
        carry_over(2 * i + 1)
        for j in range(blocks):
            k_buf[i * blocks + j] = keys[j * TILE : (j + 1) * TILE, :]
            for h in range(HEADS):
                v_buf[i * blocks + j, h, :LANES, :] = vals[
                    h * LANES : (h + 1) * LANES, j * TILE : (j + 1) * TILE
                ]

    def score(i, buf, peaks, lane, pair):
        b, k0, k1, _ = entry(lane, i)
        cols = slice(pair * PAIR, (pair + 1) * PAIR)
        q = q_ref[jnp.minimum(b, 2 * blocks - 1), pair]
        s0 = dot(k_buf[k0, :, cols], q)
        s1 = dot(k_buf[k1, :, cols], q)
        buf[lane, pair, 0] = s0
        buf[lane, pair, 1] = s1
        peaks[lane, 0:1, cols] = jnp.max(jnp.maximum(s0, s1), axis=0, keepdims=True)

    def update(i, buf, peaks, lane, pair):
        b, k0, _, v1 = entry(lane, i)
        cols = slice(pair * PAIR, (pair + 1) * PAIR)
        old = top[b, 0:1, cols]
        new = jnp.maximum(old, peaks[lane, 0:1, cols])
        scale = jnp.exp2((old - new) * factor)
        top[b, 0:1, cols] = new
        p0 = jnp.exp2((buf[lane, pair, 0] - new) * factor).astype(BF)
        p1 = jnp.exp2((buf[lane, pair, 1] - new) * factor).astype(BF)
        for side in range(2):
            h = pair * 2 + side
            sub = slice(side * LANES, (side + 1) * LANES)
            p = jnp.concatenate([p0[:, sub], p1[:, sub]], axis=0)
            v = jnp.concatenate([v_buf[k0, h], v_buf[v1, h]], axis=1)
            acc[b, h] = acc[b, h] * scale[:, sub] + dot(v, p)

    parts = [(lane, pair) for lane in range(2) for pair in range(HEADS // 2)]
    for part in parts:
        score(0, s_even, peak_even, *part)

    def two(i, carry):
        for before, part in zip(parts[-1:] + parts[:-1], parts):
            score(2 * i + 1, s_odd, peak_odd, *before)
            update(2 * i, s_even, peak_even, *part)
        for before, part in zip(parts[-1:] + parts[:-1], parts):
            score(2 * i + 2, s_even, peak_even, *before)
            update(2 * i + 1, s_odd, peak_odd, *part)
        return carry

    steps = table[base + slots]
    lax.fori_loop(0, steps >> 1, two, 0)

    @pl.when((steps & 1) == 1)
    def _():
        for part in parts:
            update(steps - 1, s_even, peak_even, *part)

    if last:
        for b in range(blocks):
            stat_ref[b, 0:1, :] = top[blocks + b, 0:1, :]
            for h in range(HEADS):
                half_ref[b, h] = acc[blocks + b, h, :LANES, :].astype(BF)
                stat_ref[b, 1:2, h * LANES : (h + 1) * LANES] = acc[
                    blocks + b, h, LANES : LANES + 1, :
                ]


def attend(slabs, group, tables, wk, wv_t, queries, factor, state, last):
    table, slots, table_width = tables
    rows, width = slabs[0].shape
    blocks = rows // TILE
    n = len(slabs)
    key_blocks = n * blocks
    first = state is None
    state_shapes = [
        jax.ShapeDtypeStruct((2 * blocks + 1, HEADS, AUG, TILE), F32),
        jax.ShapeDtypeStruct((2 * blocks + 1, 8, HEADS * LANES), F32),
    ]
    out_shape = list(state_shapes)
    if last:
        out_shape += [
            jax.ShapeDtypeStruct((blocks, HEADS, LANES, TILE), BF),
            jax.ShapeDtypeStruct((blocks, 8, HEADS * LANES), F32),
        ]
    operands = [table, *slabs, wk, wv_t, queries]
    in_specs = [whole(pltpu.SMEM)] + [whole()] * (n + 3)
    aliases = {}
    if not first:
        aliases = {len(operands) + i: i for i in range(2)}
        operands += list(state)
        in_specs += [whole()] * 2
    return pl.pallas_call(
        functools.partial(
            attend_kernel, n, group * table_width, slots, blocks, factor, first, last
        ),
        out_shape=out_shape,
        in_specs=in_specs,
        out_specs=[whole()] * len(out_shape),
        input_output_aliases=aliases,
        scratch_shapes=[
            pltpu.VMEM((key_blocks, TILE, width), BF),
            pltpu.VMEM((key_blocks + 1, HEADS, AUG, TILE), BF),
            pltpu.VMEM((2, HEADS // 2, 2, TILE, PAIR), F32),
            pltpu.VMEM((2, HEADS // 2, 2, TILE, PAIR), F32),
            pltpu.VMEM((2, 8, width), F32),
            pltpu.VMEM((2, 8, width), F32),
        ],
        compiler_params=pltpu.CompilerParams(vmem_limit_bytes=ATTEND_LIMIT << 20),
        cost_estimate=pl.CostEstimate(
            flops=n * 2_000_000_000, bytes_accessed=8 << 20, transcendentals=0
        ),
        name="attend",
    )(*operands)


def finish_kernel(
    factor,
    acc_ref,
    top_ref,
    half_ref,
    stat_ref,
    x_ref,
    wo_ref,
    wg_ref,
    wu_ref,
    wd_ref,
    out_ref,
    att,
):
    rows, _ = x_ref.shape
    for b in range(rows // TILE):
        for h in range(HEADS):
            cols = slice(h * LANES, (h + 1) * LANES)
            m1 = top_ref[b, 0:1, cols]
            m2 = stat_ref[b, 0:1, cols]
            m = jnp.maximum(m1, m2)
            a1 = jnp.exp2((m1 - m) * factor)
            a2 = jnp.exp2((m2 - m) * factor)
            den = acc_ref[b, h, LANES : LANES + 1, :] * a1 + stat_ref[b, 1:2, cols] * a2
            num = acc_ref[b, h, :LANES, :] * a1 + half_ref[b, h].astype(F32) * a2
            att[b * TILE : (b + 1) * TILE, cols] = (num / den).T.astype(BF)
    residual = x_ref[...].astype(F32) + dot(att[...], wo_ref[...])
    inverse = lax.rsqrt(jnp.mean(residual * residual, axis=-1, keepdims=True) + 1e-06)
    normed = (residual * inverse).astype(BF)
    total = residual
    ff = wg_ref.shape[1]
    for start in range(0, ff, 256):
        cols = slice(start, min(start + 256, ff))
        gate = dot(normed, wg_ref[:, cols])
        up = dot(normed, wu_ref[:, cols])
        hidden = (gate / (1.0 + jnp.exp(-gate)) * up).astype(BF)
        total = total + dot(hidden, wd_ref[cols, :])
    out_ref[...] = total.astype(BF)


def finish(mine, theirs, x, w_out, w_gate, w_up, w_down, factor):
    rows, width = x.shape
    ff = w_gate.shape[1]
    return pl.pallas_call(
        functools.partial(finish_kernel, factor),
        out_shape=jax.ShapeDtypeStruct(x.shape, BF),
        in_specs=[whole()] * 9,
        out_specs=whole(),
        scratch_shapes=[pltpu.VMEM((rows, width), BF)],
        compiler_params=pltpu.CompilerParams(vmem_limit_bytes=FINISH_LIMIT << 20),
        cost_estimate=pl.CostEstimate(
            flops=2 * rows * width * (width + 3 * ff), bytes_accessed=12 << 20, transcendentals=0
        ),
        name="finish",
    )(*mine, *theirs, x, w_out, w_gate, w_up, w_down)


def pairs(zones, devs, move):
    out = []
    for zone in range(zones):
        for dev in range(devs):
            to = move(zone, dev)
            if to is not None:
                out.append((zone * devs + dev, to[0] * devs + to[1]))
    return out


def send(x, zones, devs, move):
    return lax.ppermute(x, ("zone", "dev"), pairs(zones, devs, move))


def walks(zones, devs):
    return zones == 4 and devs == 8


def walk_plan(zone, dev):
    n, f = zone ^ 1, zone ^ 3
    return [
        [(zone, dev), (zone, dev ^ 2), (n, dev)],
        [(zone, dev ^ 4), (n, dev ^ 2), (f, dev)],
        [(zone, dev ^ 6), (n, dev ^ 4), (f, dev ^ 2)],
        [(n, dev ^ 6), (f, dev ^ 4)],
        [(f, dev ^ 6)],
    ]


def walk_links(x, x_local, zones, devs, work):
    go = functools.partial(send, zones=zones, devs=devs)
    near = lambda a: go(a, move=lambda z, d: (z ^ 1, d))
    relay = lambda a: go(a, move=lambda z, d: (z ^ 2, d))
    inner = lambda d: d // 2 in (1, 2)
    middle = lambda a: go(a, move=lambda z, d: (z, d ^ 6) if inner(d) else None)
    outer = lambda a: go(a, move=lambda z, d: (z, d ^ 2) if inner(d) else None)
    ends = lambda a: go(a, move=lambda z, d: (z, d ^ 6) if not inner(d) else None)

    a1 = go(x, move=lambda z, d: (z, d ^ 2))
    n0 = near(x)
    p2 = middle(x)
    p4 = outer(p2)
    n1 = near(a1)
    f0 = relay(n0)
    p3 = middle(a1)
    work([x_local, a1, n0])
    p5 = outer(p3)
    f1 = relay(n1)
    a2 = pick(p4, p3)
    n2 = near(a2)
    g_inner = middle(f0)
    work([a2, n1, f0])
    a3 = pick(p5, p2)
    n3 = near(a3)
    f2 = relay(n2)
    g_ends = ends(f0)
    work([a3, n2, f1])
    work([n3, f2])
    work([pick(g_ends, g_inner)])


def gather_plan(zone, dev, zones, devs):
    return [
        [(where, 2 * c + dev % 2) for c in range(start, min(start + 2, devs // 2))]
        for where in (zone, (zone - 1) % zones, (zone + 1) % zones)
        for start in range(0, devs // 2, 2)
    ]


def gather_zones(x, x_local, zones, devs, work):
    chips = devs // 2
    ahead = lax.ppermute(x, "zone", [(i, (i + 1) % zones) for i in range(zones)])
    behind = lax.ppermute(x, "zone", [((i + 1) % zones, i) for i in range(zones)])
    same_core = [[d for d in range(devs) if d % 2 == c] for c in range(2)]
    for slab in (x, ahead, behind):
        every = lax.all_gather(slab, "dev", axis=0, axis_index_groups=same_core)
        for start in range(0, chips, 2):
            work([every[c] for c in range(start, min(start + 2, chips))])


def body(
    node_features,
    neighbour_blocks,
    neighbour_count,
    tile_valid,
    w_query,
    w_key,
    w_value,
    w_out,
    w_gate,
    w_up,
    w_down,
):
    _, width = node_features.shape
    zones, devs = lax.axis_size("zone"), lax.axis_size("dev")
    factor = math.log2(math.e) / math.sqrt(width // HEADS)
    go = functools.partial(send, zones=zones, devs=devs)
    swap = lambda a: go(a, move=lambda z, d: (z, d ^ 1))

    partner = swap(node_features)
    listed = swap(neighbour_blocks)
    if walks(zones, devs):
        plan, run = walk_plan, walk_links
    else:
        plan, run = functools.partial(gather_plan, zones=zones, devs=devs), gather_zones
    sizes = [len(group) for group in plan(0, 0)]
    tables, queries, wv_t, x_local, wk_local = prepare(
        plan,
        sizes,
        neighbour_count,
        tile_valid,
        neighbour_blocks,
        listed,
        node_features,
        partner,
        w_query,
        w_value,
        w_key,
    )
    state, turn = None, 0

    def work(slabs):
        nonlocal state, turn
        last = turn == len(sizes) - 1
        state = attend(slabs, turn, tables, wk_local, wv_t, queries, factor, state, last)
        turn += 1

    run(node_features, x_local, zones, devs, work)
    theirs = [swap(state[2]), swap(state[3])]
    return finish(state[:2], theirs, node_features, w_out, w_gate, w_up, w_down, factor)


def solution(mesh):
    placed = (
        P(("zone", "dev"), None),
        P(("zone", "dev"), None),
        P(("zone", "dev")),
        P(),
        P(),
        P(),
        P(),
        P(),
        P(),
        P(),
        P(),
    )

    return jax.shard_map(
        body, mesh=mesh, in_specs=placed, out_specs=P(("zone", "dev"), None), check_vma=False
    )
```
